512 devices in a mesh: dp: 16 (over z, core), tensor: 32 (over x, y).
Axes of the slice: x: 4, y: 8, z: 8, core: 2. Of those that a mesh axis runs over, the one named last changes fastest.
Arguments:
- q_rows: bfloat16 [1024, 4096], P('dp', 'tensor'), parts along dimension 0, may hold values from -160 to 160, as said below
- k_cache: bfloat16 [64, 8192, 512], P('dp', 'tensor'), parts along dimension 0, may hold values from -6 to 6
- v_cache: bfloat16 [64, 8192, 512], P('dp', 'tensor'), parts along dimension 0, may hold values from -24 to 24
- k_tree: bfloat16 [64, 16, 512], P('dp'), parts along dimension 0, may hold values from -18 to 18
- v_tree: bfloat16 [64, 16, 512], P('dp'), parts along dimension 0, may hold values from -24 to 24
- residual: bfloat16 [1024, 8192], P('dp', 'tensor'), parts along dimension 0, may hold values from -2 to 2
- wo_rows: bfloat16 [4096, 8192], P('tensor'), may hold values from -1 to 1
- gain: bfloat16 [8192], P('tensor'), may hold values from 0.099609375 to 1.8984375
- parents: int32 [64, 16], P('dp'), parts along dimension 0, may hold values from 0 to 6, as said below
- cache_len: int32 [64], P('dp'), parts along dimension 0, may hold values from 1024 to 8192, as said below
- accepted_node: int32 [64], P('dp'), parts along dimension 0, may hold values from 0 to 15, as said below
Outputs:
- layer_out: bfloat16 [1024, 8192], P('dp', 'tensor'), parts along dimension 0
- draft_feat: bfloat16 [64, 8, 8192], P('dp', None, 'tensor'), parts along dimension 0
The draws below stay inside these ranges and needn't reach their ends.
There are 16 independent parts, one for each index of `dp`. The reference program is written for one: setup_inputs(seed, part) draws one part's arguments, and reference() takes and returns one part's arrays. A program takes and returns all parts, laid end to end along the dimension named above; an argument that names none is the same for every part. Nothing has to cross between parts.
Inputs may be any that keep to these rules, and one draw needn't show every extreme that they name: `q_rows`: float queries of order one; in the hidden draw some rows are scaled up strongly. `parents`: nodes 1 to 7 form a chain (parent of node i is i - 1); every later node has a parent below 7; entry 0 is 0. `cache_len`: in every group some request has all 8192 positions valid. `accepted_node`: in every group some request accepts node 7, whose path holds 8 nodes.
All inputs are finite; a program needn't handle non-finite values.
Results may differ from the reference program's by a relative error of at most 0.0075.
Values may be sent and summed in bfloat16 or wider, within the bound.
No kernel may reach another device: no remote copies, remote signals or barrier semaphores. Data moves between devices by JAX's collectives and lax.ppermute only.
A program may use at most 64 MiB of HBM per device.

```python
import jax
import jax.numpy as jnp
from jax import lax

D = 8192
HD = 128
HEADS_DEV = 1
KVH = 4
REQ = 4
TREE = 16
MAXACC = 8
HEADS = 32
CACHE = 8192
ROWS = 64


def draw_q_rows(key, part):
    base = jax.random.truncated_normal(key, -4.0, 4.0, (ROWS, HEADS * HD), jnp.float32)
    return base.astype(jnp.bfloat16)


def value_offsets(key):
    means = jax.random.uniform(jax.random.fold_in(key, 23), (HD,), jnp.float32, 0.3, 1.0)
    return jnp.tile(means, KVH)


def value_noise(key, shape):
    noise = 4.0 * jax.random.truncated_normal(key, -5.75, 5.75, shape, jnp.float32)
    return noise


def draw_v_cache(key, part):
    noise = value_noise(jax.random.fold_in(key, 21), (REQ, CACHE, KVH * HD))
    return (noise + value_offsets(key)[None, None, :]).astype(jnp.bfloat16)


def draw_v_tree(key, part):
    noise = value_noise(jax.random.fold_in(key, 22), (REQ, TREE, KVH * HD))
    return (noise + value_offsets(key)[None, None, :]).astype(jnp.bfloat16)


def draw_wo_rows(key, part):
    fan = HEADS * HD
    tensor_count = HEADS // HEADS_DEV
    row_block = jnp.arange(fan, dtype=jnp.int32) // (HEADS_DEV * HD)
    col_block = jnp.arange(D, dtype=jnp.int32) // (D // tensor_count)
    pairing = jax.random.permutation(jax.random.fold_in(key, 41), tensor_count).astype(jnp.int32)
    boost = jnp.where(pairing[row_block][:, None] == col_block[None, :], 3.0, 1.0)
    noise = jax.random.truncated_normal(key, -3.0, 3.0, (fan, D), jnp.float32)
    signs = (2 * jax.random.randint(jax.random.fold_in(key, 42), (D,), 0, 2) - 1).astype(jnp.float32)
    return (noise * boost * fan ** (-0.5) + signs[None, :] * (1.5 / fan)).astype(jnp.bfloat16)


def draw_parents(key, part):
    nodes = jnp.arange(TREE, dtype=jnp.int32)
    later = jax.random.randint(key, (REQ, TREE), 0, MAXACC - 1)
    chain = jnp.maximum(nodes - 1, 0)
    return jnp.where(nodes[None, :] < MAXACC, chain[None, :], later).astype(jnp.int32)


def draw_cache_len(key, part):
    lengths = jax.random.randint(key, (REQ,), CACHE // 8, CACHE + 1)
    fullest = jax.random.randint(jax.random.fold_in(key, 5), (), 0, REQ)
    return jnp.where(jnp.arange(REQ, dtype=jnp.int32) == fullest, CACHE, lengths).astype(jnp.int32)


def draw_accepted_node(key, part):
    chosen = jax.random.randint(key, (REQ,), 0, TREE)
    deepest = jax.random.randint(jax.random.fold_in(key, 9), (), 0, REQ)
    return jnp.where(jnp.arange(REQ, dtype=jnp.int32) == deepest, MAXACC - 1, chosen).astype(jnp.int32)


def shard_levels(stream_key, shape, pieces, smallest, high):
    level, own = 1.0, jax.random.fold_in(stream_key, 6)
    for dim, blocks in pieces:
        heights = jnp.exp(jax.random.uniform(jax.random.fold_in(own, dim), (blocks,), jnp.float32, smallest / len(pieces), high / len(pieces)))
        level = level * jnp.repeat(heights, shape[dim] // blocks).reshape([-1 if axis == dim else 1 for axis in range(len(shape))])
    return level


def scatter_about(stream_key, shape, scale, bound, pieces=(), kind=jnp.bfloat16):
    entries = scale * jax.random.normal(stream_key, shape, jnp.float32)
    if pieces:
        entries = entries * shard_levels(stream_key, shape, pieces, -0.22, 0.18)
    return jnp.clip(entries, -bound, bound).astype(kind)


def setup_inputs(seed: int = 0, part: int = 0) -> dict:
    arg_keys = jax.random.split(jax.random.key(seed), 12)
    own_keys = jax.random.split(jax.random.fold_in(arg_keys[11], part), 12)
    return {
        "q_rows": draw_q_rows(jax.random.fold_in(jax.random.fold_in(arg_keys[11], part), 71), part),
        "k_cache": scatter_about(own_keys[1], (REQ, CACHE, KVH * HD), 1.0, 6.0, ((1, 32),)),
        "v_cache": draw_v_cache(jax.random.fold_in(jax.random.fold_in(arg_keys[11], part), 71), part),
        "k_tree": scatter_about(own_keys[3], (REQ, TREE, KVH * HD), 3.0, 18.0),
        "v_tree": draw_v_tree(jax.random.fold_in(jax.random.fold_in(arg_keys[11], part), 71), part),
        "residual": scatter_about(own_keys[5], (ROWS, D), 0.3, 2.0, ((1, 32),)),
        "wo_rows": draw_wo_rows(jax.random.fold_in(arg_keys[11], 71), part),
        "gain": jnp.clip(1.0 + 0.18 * jax.random.normal(arg_keys[7], (D,), jnp.float32), 0.099609375, 1.8984375).astype(jnp.bfloat16),
        "parents": draw_parents(jax.random.fold_in(jax.random.fold_in(arg_keys[11], part), 71), part),
        "cache_len": draw_cache_len(jax.random.fold_in(jax.random.fold_in(arg_keys[11], part), 71), part),
        "accepted_node": draw_accepted_node(jax.random.fold_in(jax.random.fold_in(arg_keys[11], part), 71), part),
    }


floor_score = -1e+30
epsilon = 1e-05

def ancestors(parents):
    nodes = jnp.arange(TREE, dtype=jnp.int32)
    link = (parents[:, :, None] == nodes[None, None, :]) & (nodes[None, :, None] > 0)
    reach = jnp.minimum(jnp.eye(TREE, dtype=jnp.float32)[None] + link.astype(jnp.float32), 1.0)
    for sweep in range((TREE - 1).bit_length()):
        reach = jnp.minimum(jnp.einsum('rab,rbc->rac', reach, reach, precision=lax.Precision.HIGHEST), 1.0)
    return reach

def path_select(reach, accepted_node):
    depth = lax.optimization_barrier(jnp.sum(reach, axis=2)) - 1.0
    onehot = (jnp.arange(TREE, dtype=jnp.int32)[None, :] == accepted_node[:, None]).astype(jnp.float32)
    onpath = jnp.einsum('rt,rtu->ru', onehot, reach, precision=lax.Precision.HIGHEST)
    levels = jnp.arange(MAXACC).astype(jnp.float32)
    return onpath[:, None, :] * (depth[:, None, :] == levels[None, :, None]).astype(jnp.float32)

def reference(q_rows, k_cache, v_cache, k_tree, v_tree, residual, wo_rows, gain, parents, cache_len, accepted_node):
    group_size = HEADS // KVH
    score_scale = HD ** (-0.5)
    highest = lax.Precision.HIGHEST
    q_view = q_rows.astype(jnp.float32).reshape(REQ, TREE, KVH, group_size, HD)
    cache_keys = k_cache.astype(jnp.float32).reshape(REQ, CACHE, KVH, HD)
    cache_values = v_cache.astype(jnp.float32).reshape(REQ, CACHE, KVH, HD)
    tree_keys = k_tree.astype(jnp.float32).reshape(REQ, TREE, KVH, HD)
    tree_values = v_tree.astype(jnp.float32).reshape(REQ, TREE, KVH, HD)
    reach = ancestors(parents)
    cache_scores = jnp.einsum('rtkgd,rckd->kgrtc', q_view, cache_keys, precision=highest) * score_scale
    valid = (jnp.arange(CACHE, dtype=jnp.int32)[None, :] < cache_len[:, None])[None, None, :, None, :]
    cache_scores = jnp.where(valid, cache_scores, floor_score)
    tree_scores = jnp.einsum('rtkgd,rukd->kgrtu', q_view, tree_keys, precision=highest) * score_scale
    tree_valid = (reach > 0.5)[None, None]
    tree_scores = jnp.where(tree_valid, tree_scores, floor_score)
    top = jnp.maximum(lax.optimization_barrier(jnp.max(cache_scores, axis=4)), lax.optimization_barrier(jnp.max(tree_scores, axis=4)))
    cache_weights = jnp.where(valid, jnp.exp(cache_scores - top[..., None]), 0.0)
    tree_weights = jnp.where(tree_valid, jnp.exp(tree_scores - top[..., None]), 0.0)
    denominator = lax.optimization_barrier(jnp.sum(cache_weights, axis=4)) + lax.optimization_barrier(jnp.sum(tree_weights, axis=4))
    total = jnp.einsum('kgrtc,rckd->kgrtd', cache_weights.astype(jnp.bfloat16).astype(jnp.float32), cache_values, precision=highest)
    total = total + jnp.einsum('kgrtu,rukd->kgrtd', tree_weights.astype(jnp.bfloat16).astype(jnp.float32), tree_values, precision=highest)
    attention = (total / denominator[..., None]).astype(jnp.bfloat16)
    attention = jnp.transpose(attention, (2, 3, 0, 1, 4)).reshape(ROWS, HEADS * HD)
    hidden = residual.astype(jnp.float32) + jnp.dot(attention, wo_rows, preferred_element_type=jnp.float32)
    layer_out = hidden.astype(jnp.bfloat16)
    mean_square = lax.optimization_barrier(jnp.mean(hidden * hidden, axis=1))
    features = (hidden * lax.rsqrt(mean_square + epsilon)[:, None] * gain.astype(jnp.float32)[None, :]).astype(jnp.bfloat16)
    select = path_select(reach, accepted_node)
    draft_feat = jnp.einsum('rat,rtc->rac', select, features.astype(jnp.float32).reshape(REQ, TREE, D), precision=highest)
    return (layer_out, draft_feat.astype(jnp.bfloat16))
```

```python
import jax
import jax.numpy as jnp
from jax import lax
from jax.experimental import pallas as pl
from jax.experimental.pallas import tpu as pltpu
from jax.sharding import PartitionSpec as P

D = 8192
HD = 128
KVH = 4
TREE = 16
REQ = 4
ROWS = REQ * TREE
MAXACC = 8
HEADS = 32
GROUP = HEADS // KVH
STAT = 8
MSG = ROWS + STAT

floor_score = -1e30
epsilon = 1e-05
score_scale = HD ** (-0.5)
f32 = jnp.float32
bf16 = jnp.bfloat16
VM = pl.BlockSpec(memory_space=pltpu.VMEM)
SM = pl.BlockSpec(memory_space=pltpu.SMEM)


def iota(shape, dim):
    return lax.broadcasted_iota(jnp.int32, shape, dim)


def three_parts(x):
    hi = x.astype(bf16).astype(f32)
    mid = (x - hi).astype(bf16).astype(f32)
    return hi, mid, x - hi - mid


def to_all(x):
    return lax.all_to_all(x, "tensor", split_axis=0, concat_axis=0, tiled=True)


def tree_kernel(rank, parents, q, kt, vt, acc_node, o_ref, lse_ref, sel_ref):
    row = iota((ROWS, ROWS), 0)
    col = iota((ROWS, ROWS), 1)
    same = (row // TREE) == (col // TREE)
    up = jnp.zeros((ROWS, ROWS), jnp.int32)
    for r in range(REQ):
        for i in range(1, TREE):
            up = jnp.where(row == r * TREE + i, parents[r, i] + r * TREE, up)
    link = jnp.where((up == col) & (row % TREE > 0), 1.0, 0.0)
    reach = jnp.where(row == col, 1.0, link)
    for sweep in range((TREE - 1).bit_length()):
        half = reach.astype(bf16)
        reach = jnp.minimum(jnp.dot(half, half, preferred_element_type=f32), 1.0)
    lane = pl.ds(pl.multiple_of((rank[0] // GROUP) * HD, HD), HD)
    keys = jnp.concatenate([kt[r, :, lane] for r in range(REQ)], axis=0)
    values = jnp.concatenate([vt[r, :, lane] for r in range(REQ)], axis=0)
    nt = (((1,), (1,)), ((), ()))
    scores = lax.dot_general(q[...], keys, nt, preferred_element_type=f32) * score_scale
    valid = (reach > 0.5) & same
    scores = jnp.where(valid, scores, floor_score)
    top = jnp.max(scores, axis=1, keepdims=True)
    e = jnp.where(valid, jnp.exp(scores - top), 0.0)
    total = jnp.sum(e, axis=1, keepdims=True)
    o_ref[...] = jnp.dot(e.astype(bf16), values, preferred_element_type=f32) / total
    lse = jnp.broadcast_to(top + jnp.log(total), (ROWS, HD))
    lse_ref[...] = lse.T[:8, :]
    depth = lax.dot_general(
        jnp.ones((8, ROWS), bf16), reach.astype(bf16), nt, preferred_element_type=f32
    )[:1, :] - 1.0
    out = iota((REQ * MAXACC, ROWS), 0)
    lanes = iota((REQ * MAXACC, ROWS), 1)
    chosen = jnp.zeros((REQ * MAXACC, ROWS), jnp.int32)
    for r in range(REQ):
        chosen = jnp.where(out // MAXACC == r, acc_node[r] + r * TREE, chosen)
    onehot = jnp.where(lanes == chosen, 1.0, 0.0).astype(bf16)
    onpath = jnp.dot(onehot, reach.astype(bf16), preferred_element_type=f32)
    level = (out % MAXACC).astype(f32)
    sel_ref[...] = jnp.where(depth == level, onpath, 0.0).astype(bf16)


def attend_kernel(rank, cache_len, q, k, v, out):
    span = k.shape[1]
    nt = (((1,), (1,)), ((), ()))
    tn = (((0,), (0,)), ((), ()))
    start = rank[0] * span
    pos = iota((span, HD), 0) + start
    sub = iota((GROUP, HD), 0)
    lane = iota((GROUP, HD), 1)
    for g in range(KVH):
        cols = slice(g * HD, (g + 1) * HD)
        packed = jnp.zeros((GROUP, HD), f32)
        for r in range(REQ):
            rows = slice(r * TREE, (r + 1) * TREE)
            qh = q[g * GROUP : (g + 1) * GROUP, rows, :].reshape(GROUP * TREE, HD)
            s = lax.dot_general(k[r, :, cols], qh, nt, preferred_element_type=f32) * score_scale
            valid = pos < cache_len[r]
            s = jnp.where(valid, s, floor_score)
            top = jnp.max(s, axis=0, keepdims=True)
            e = jnp.where(valid, jnp.exp(s - top), 0.0)
            total = jnp.sum(e, axis=0, keepdims=True)
            some = total > 0.0
            inv = jnp.where(some, 1.0 / jnp.where(some, total, 1.0), 0.0)
            lse = jnp.where(some, top + jnp.log(jnp.where(some, total, 1.0)), floor_score)
            p = (e * inv).astype(bf16)
            o = lax.dot_general(p, v[r, :, cols], tn, preferred_element_type=f32)
            out[g * GROUP : (g + 1) * GROUP, rows, :] = o.astype(bf16).reshape(GROUP, TREE, HD)
            turned = pltpu.roll(
                jnp.broadcast_to(pltpu.roll(lse, (r + 1) * TREE, 1), (GROUP, HD)),
                0,
                1,
                stride=TREE,
                stride_axis=0,
            )
            packed = jnp.where(lane // TREE == r, turned, packed)
        hi, mid, lo = three_parts(packed)
        first = jnp.where(lane < ROWS, hi, pltpu.roll(mid, ROWS, 1))
        for j in range(GROUP):
            i = GROUP - 1 - j
            stat = jnp.where(sub == 0, first[i : i + 1, :], jnp.where(sub == 1, lo[i : i + 1, :], 0.0))
            out[g * GROUP + j, ROWS:MSG, :] = stat.astype(bf16)


def project_kernel(got, o_tree, lse_tree, wo, out):
    srcs = got.shape[0]
    stats = got[:, ROWS:MSG, :].astype(f32)
    first = stats[:, 0, :]
    lse = first + pltpu.roll(first, ROWS, 1) + stats[:, 1, :]
    tree = lse_tree[0:1, :]
    tree = jnp.concatenate([tree, jnp.zeros((1, HD - ROWS), f32)], axis=1)
    top = jnp.maximum(jnp.max(lse, axis=0, keepdims=True), tree)
    w = jnp.exp(lse - top)
    wt = jnp.exp(tree - top)
    inv = 1.0 / (jnp.sum(w, axis=0, keepdims=True) + wt)
    every = jnp.concatenate(
        [w * inv, jnp.broadcast_to(wt * inv, (8, HD)), jnp.zeros((HD - srcs - 8, HD), f32)], axis=0
    ).T[:ROWS, :]
    att = o_tree[...] * every[:, srcs : srcs + 1]
    for c in range(srcs):
        att = att + got[c, :ROWS, :].astype(f32) * every[:, c : c + 1]
    att = att.astype(bf16)
    width = out.shape[2]
    for d in range(out.shape[0]):
        part = jnp.dot(att, wo[:, d * width : (d + 1) * width], preferred_element_type=f32)
        out[d] = part.astype(bf16)


def hidden_kernel(got, residual, h_ref, layer_ref, sq_ref):
    h = residual[...].astype(f32)
    for c in range(got.shape[0]):
        h = h + got[c].astype(f32)
    h_ref[...] = h
    layer_ref[...] = h.astype(bf16)
    sq = lax.dot_general(
        jnp.ones((8, h.shape[1]), f32),
        h * h,
        (((1,), (1,)), ((), ())),
        preferred_element_type=f32,
        precision=lax.Precision.HIGHEST,
    )
    sq_ref[...] = jnp.broadcast_to(sq[0:1, :][None], sq_ref.shape)


def draft_kernel(got, h, gain, sel, out):
    sq = got[...].reshape(got.shape[0], ROWS)
    total = lax.dot_general(
        sq,
        jnp.ones((got.shape[0], h.shape[1]), f32),
        (((0,), (0,)), ((), ())),
        preferred_element_type=f32,
        precision=lax.Precision.HIGHEST,
    )
    scale = lax.rsqrt(total / D + epsilon)
    feat = (h[...] * scale * gain[...].astype(f32)).astype(bf16)
    out[...] = jnp.dot(sel[...], feat, preferred_element_type=f32).astype(bf16)


def shape(dims, kind):
    return jax.ShapeDtypeStruct(dims, kind)


def on_device(
    q_rows,
    k_cache,
    v_cache,
    k_tree,
    v_tree,
    residual,
    wo_rows,
    gain,
    parents,
    cache_len,
    accepted_node,
):
    count = lax.axis_size("tensor")
    rank = lax.axis_index("tensor").astype(jnp.int32).reshape(1)
    width = residual.shape[1]
    q_all = to_all(jnp.broadcast_to(q_rows, (count, ROWS, HD)))
    o_tree, lse_tree, sel = pl.pallas_call(
        tree_kernel,
        name="tree",
        out_shape=(shape((ROWS, HD), f32), shape((8, ROWS), f32), shape((REQ * MAXACC, ROWS), bf16)),
        in_specs=[SM, SM, VM, VM, VM, SM],
        out_specs=(VM, VM, VM),
        cost_estimate=pl.CostEstimate(flops=10**8, bytes_accessed=300000, transcendentals=10000),
    )(rank, parents, q_rows, k_tree, v_tree, accepted_node)
    sent = pl.pallas_call(
        attend_kernel,
        name="attend",
        out_shape=shape((HEADS, MSG, HD), bf16),
        in_specs=[SM, SM, VM, VM, VM],
        out_specs=VM,
    )(rank, cache_len, q_all, k_cache, v_cache)
    got = to_all(sent)
    terms = pl.pallas_call(
        project_kernel,
        name="project",
        out_shape=shape((count, ROWS, width), bf16),
        in_specs=[VM, VM, VM, VM],
        out_specs=VM,
    )(got, o_tree, lse_tree, wo_rows)
    arrived = to_all(terms)
    h, layer_out, squares = pl.pallas_call(
        hidden_kernel,
        name="hidden",
        out_shape=(shape((ROWS, width), f32), shape((ROWS, width), bf16), shape((count, 1, ROWS), f32)),
        in_specs=[VM, VM],
        out_specs=(VM, VM, VM),
    )(arrived, residual)
    totals = to_all(squares)
    draft = pl.pallas_call(
        draft_kernel,
        name="draft",
        out_shape=shape((REQ * MAXACC, width), bf16),
        in_specs=[VM, VM, VM, VM],
        out_specs=VM,
    )(totals, h, gain.reshape(1, width), sel)
    return (layer_out, draft.reshape(REQ, MAXACC, width))


def solution(mesh):
    return jax.shard_map(
        on_device,
        mesh=mesh,
        in_specs=(
            P("dp", "tensor"),
            P("dp", "tensor", None),
            P("dp", "tensor", None),
            P("dp", None, None),
            P("dp", None, None),
            P("dp", "tensor"),
            P("tensor", None),
            P("tensor"),
            P("dp", None),
            P("dp"),
            P("dp"),
        ),
        out_specs=(P("dp", "tensor"), P("dp", None, "tensor")),
        check_vma=False,
    )
```

```python
import jax
import jax.numpy as jnp
from jax import lax
from jax.experimental import pallas as pl
from jax.experimental.pallas import tpu as pltpu
from jax.sharding import PartitionSpec as P

D = 8192
HD = 128
KVH = 4
TREE = 16
REQ = 4
ROWS = REQ * TREE
MAXACC = 8
HEADS = 32
GROUP = HEADS // KVH
STAT = 8
MSG = ROWS + STAT

floor_score = -1e30
epsilon = 1e-05
score_scale = HD ** (-0.5)
f32 = jnp.float32
bf16 = jnp.bfloat16
VM = pl.BlockSpec(memory_space=pltpu.VMEM)
SM = pl.BlockSpec(memory_space=pltpu.SMEM)
STAGGER = 12000


def iota(shape, dim):
    return lax.broadcasted_iota(jnp.int32, shape, dim)


def three_parts(x):
    hi = x.astype(bf16).astype(f32)
    mid = (x - hi).astype(bf16).astype(f32)
    return hi, mid, x - hi - mid


def to_all(x):
    return lax.all_to_all(x, "tensor", split_axis=0, concat_axis=0, tiled=True)


def spread_kernel(late, q, out):
    @pl.when(late[0] > 0)
    def _():
        pl.delay(STAGGER)

    for d in range(out.shape[0]):
        out[d] = q[...]


def tree_kernel(
    rank, parents, acc_node, cache_len, q, kt, vt, k, v, o_ref, lse_ref, sel_ref, left_ref
):
    for r in range(REQ):
        left_ref[r] = jnp.full((8, HD), cache_len[r] - rank[0] * k.shape[1], jnp.int32)
    row = iota((ROWS, ROWS), 0)
    col = iota((ROWS, ROWS), 1)
    same = (row // TREE) == (col // TREE)
    up = jnp.zeros((ROWS, ROWS), jnp.int32)
    for r in range(REQ):
        for i in range(1, TREE):
            up = jnp.where(row == r * TREE + i, parents[r, i] + r * TREE, up)
    link = jnp.where((up == col) & (row % TREE > 0), 1.0, 0.0)
    reach = jnp.where(row == col, 1.0, link)
    for sweep in range((TREE - 1).bit_length()):
        half = reach.astype(bf16)
        reach = jnp.minimum(jnp.dot(half, half, preferred_element_type=f32), 1.0)
    lane = pl.ds(pl.multiple_of((rank[0] // GROUP) * HD, HD), HD)
    keys = jnp.concatenate([kt[r, :, lane] for r in range(REQ)], axis=0)
    values = jnp.concatenate([vt[r, :, lane] for r in range(REQ)], axis=0)
    nt = (((1,), (1,)), ((), ()))
    scores = lax.dot_general(q[...], keys, nt, preferred_element_type=f32) * score_scale
    valid = (reach > 0.5) & same
    scores = jnp.where(valid, scores, floor_score)
    top = jnp.max(scores, axis=1, keepdims=True)
    e = jnp.where(valid, jnp.exp(scores - top), 0.0)
    total = jnp.sum(e, axis=1, keepdims=True)
    o_ref[...] = jnp.dot(e.astype(bf16), values, preferred_element_type=f32) / total
    lse = jnp.broadcast_to(top + jnp.log(total), (ROWS, HD))
    lse_ref[...] = lse.T[:8, :]
    depth = lax.dot_general(
        jnp.ones((8, ROWS), bf16), reach.astype(bf16), nt, preferred_element_type=f32
    )[:1, :] - 1.0
    out = iota((REQ * MAXACC, ROWS), 0)
    lanes = iota((REQ * MAXACC, ROWS), 1)
    chosen = jnp.zeros((REQ * MAXACC, ROWS), jnp.int32)
    for r in range(REQ):
        chosen = jnp.where(out // MAXACC == r, acc_node[r] + r * TREE, chosen)
    onehot = jnp.where(lanes == chosen, 1.0, 0.0).astype(bf16)
    onpath = jnp.dot(onehot, reach.astype(bf16), preferred_element_type=f32)
    level = (out % MAXACC).astype(f32)
    sel_ref[...] = jnp.where(depth == level, onpath, 0.0).astype(bf16)


def attend_kernel(left, q, k, v, out):
    span = k.shape[1]
    nt = (((1,), (1,)), ((), ()))
    tn = (((0,), (0,)), ((), ()))
    pos = iota((span, HD), 0)
    sub = iota((GROUP, HD), 0)
    lane = iota((GROUP, HD), 1)
    packed = [jnp.zeros((GROUP, HD), f32)] * KVH
    for r in range(REQ):
        rows = slice(r * TREE, (r + 1) * TREE)
        valid = pos < left[r, 0:1, :]
        for g in range(KVH):
            cols = slice(g * HD, (g + 1) * HD)
            heads = slice(g * GROUP, (g + 1) * GROUP)
            qh = q[heads, rows, :].reshape(GROUP * TREE, HD)
            s = lax.dot_general(k[r, :, cols], qh, nt, preferred_element_type=f32) * score_scale
            s = jnp.where(valid, s, floor_score)
            top = jnp.max(s, axis=0, keepdims=True)
            e = jnp.where(valid, jnp.exp(s - top), 0.0)
            total = jnp.sum(e, axis=0, keepdims=True)
            some = total > 0.0
            inv = jnp.where(some, 1.0 / jnp.where(some, total, 1.0), 0.0)
            lse = jnp.where(some, top + jnp.log(jnp.where(some, total, 1.0)), floor_score)
            p = (e * inv).astype(bf16)
            o = lax.dot_general(p, v[r, :, cols], tn, preferred_element_type=f32)
            out[heads, rows, :] = o.astype(bf16).reshape(GROUP, TREE, HD)
            turned = pltpu.roll(
                jnp.broadcast_to(pltpu.roll(lse, (r + 1) * TREE, 1), (GROUP, HD)),
                0,
                1,
                stride=TREE,
                stride_axis=0,
            )
            packed[g] = jnp.where(lane // TREE == r, turned, packed[g])
    for g in range(KVH):
        hi, mid, lo = three_parts(packed[g])
        first = jnp.where(lane < ROWS, hi, pltpu.roll(mid, ROWS, 1))
        for j in range(GROUP):
            i = GROUP - 1 - j
            stat = jnp.where(sub == 0, first[i : i + 1, :], jnp.where(sub == 1, lo[i : i + 1, :], 0.0))
            out[g * GROUP + j, ROWS:MSG, :] = stat.astype(bf16)


def project_kernel(got, o_tree, lse_tree, wo, out):
    srcs = got.shape[0]
    stats = got[:, ROWS:MSG, :].astype(f32)
    first = stats[:, 0, :]
    lse = first + pltpu.roll(first, ROWS, 1) + stats[:, 1, :]
    tree = lse_tree[0:1, :]
    tree = jnp.concatenate([tree, jnp.zeros((1, HD - ROWS), f32)], axis=1)
    top = jnp.maximum(jnp.max(lse, axis=0, keepdims=True), tree)
    w = jnp.exp(lse - top)
    wt = jnp.exp(tree - top)
    inv = 1.0 / (jnp.sum(w, axis=0, keepdims=True) + wt)
    every = jnp.concatenate(
        [w * inv, jnp.broadcast_to(wt * inv, (8, HD)), jnp.zeros((HD - srcs - 8, HD), f32)], axis=0
    ).T[:ROWS, :]
    att = o_tree[...] * every[:, srcs : srcs + 1]
    for c in range(srcs):
        att = att + got[c, :ROWS, :].astype(f32) * every[:, c : c + 1]
    att = att.astype(bf16)
    width = out.shape[2]
    for d in range(out.shape[0]):
        part = jnp.dot(att, wo[:, d * width : (d + 1) * width], preferred_element_type=f32)
        out[d] = part.astype(bf16)


def hidden_kernel(got, residual, h_ref, layer_ref, sq_ref):
    h = residual[...].astype(f32)
    for c in range(got.shape[0]):
        h = h + got[c].astype(f32)
    h_ref[...] = h
    layer_ref[...] = h.astype(bf16)
    sq = h * h
    part = sq[:, :HD]
    for c in range(HD, sq.shape[1], HD):
        part = part + sq[:, c : c + HD]
    row = jnp.sum(part.T, axis=0, keepdims=True)
    row = jnp.concatenate([row, jnp.zeros((1, HD - ROWS), f32)], axis=1)
    hi, mid, lo = three_parts(row)
    sub = iota((STAT, HD), 0)
    tile = jnp.where(sub == 0, hi, jnp.where(sub == 1, mid, jnp.where(sub == 2, lo, 0.0))).astype(bf16)
    for c in range(sq_ref.shape[0]):
        sq_ref[c] = tile


def draft_kernel(got, h, gain, sel, out):
    tile = got[0].astype(f32)
    for c in range(1, got.shape[0]):
        tile = tile + got[c].astype(f32)
    total = jnp.sum(tile, axis=0, keepdims=True)
    scale = lax.rsqrt(jnp.broadcast_to(total / D, (HD, HD)).T[:ROWS, :] + epsilon)
    for c in range(0, h.shape[1], HD):
        cols = slice(c, c + HD)
        feat = (h[:, cols] * scale * gain[:, cols].astype(f32)).astype(bf16)
        out[:, cols] = jnp.dot(sel[...], feat, preferred_element_type=f32).astype(bf16)


def params(mib):
    return pltpu.CompilerParams(vmem_limit_bytes=mib * 2**20)


def shape(dims, kind):
    return jax.ShapeDtypeStruct(dims, kind)


def on_device(
    q_rows,
    k_cache,
    v_cache,
    k_tree,
    v_tree,
    residual,
    wo_rows,
    gain,
    parents,
    cache_len,
    accepted_node,
):
    count = lax.axis_size("tensor")
    rank = lax.axis_index("tensor").astype(jnp.int32).reshape(1)
    width = residual.shape[1]
    q_each = pl.pallas_call(
        spread_kernel,
        name="spread",
        compiler_params=params(2),
        out_shape=shape((count, ROWS, HD), bf16),
        in_specs=[SM, VM],
        out_specs=VM,
    )(lax.axis_index("dp").astype(jnp.int32).reshape(1) % 2, q_rows)
    q_all = to_all(q_each)
    o_tree, lse_tree, sel, left = pl.pallas_call(
        tree_kernel,
        name="tree",
        compiler_params=params(6),
        out_shape=(
            shape((ROWS, HD), f32),
            shape((8, ROWS), f32),
            shape((REQ * MAXACC, ROWS), bf16),
            shape((REQ, 8, HD), jnp.int32),
        ),
        in_specs=[SM, SM, SM, SM, VM, VM, VM, VM, VM],
        out_specs=(VM, VM, VM, VM),
        cost_estimate=pl.CostEstimate(flops=10**8, bytes_accessed=4 * 10**6, transcendentals=10000),
    )(rank, parents, accepted_node, cache_len, q_rows, k_tree, v_tree, k_cache, v_cache)
    sent = pl.pallas_call(
        attend_kernel,
        name="attend",
        compiler_params=params(10),
        out_shape=shape((HEADS, MSG, HD), bf16),
        in_specs=[VM, VM, VM, VM],
        out_specs=VM,
    )(left, q_all, k_cache, v_cache)
    got = to_all(sent)
    terms = pl.pallas_call(
        project_kernel,
        name="project",
        compiler_params=params(10),
        out_shape=shape((count, ROWS, width), bf16),
        in_specs=[VM, VM, VM, VM],
        out_specs=VM,
    )(got, o_tree, lse_tree, wo_rows)
    arrived = to_all(terms)
    h, layer_out, squares = pl.pallas_call(
        hidden_kernel,
        name="hidden",
        compiler_params=params(6),
        out_shape=(shape((ROWS, width), f32), shape((ROWS, width), bf16), shape((count, STAT, HD), bf16)),
        in_specs=[VM, VM],
        out_specs=(VM, VM, VM),
    )(arrived, residual)
    totals = to_all(squares)
    draft = pl.pallas_call(
        draft_kernel,
        name="draft",
        compiler_params=params(4),
        out_shape=shape((REQ * MAXACC, width), bf16),
        in_specs=[VM, VM, VM, VM],
        out_specs=VM,
    )(totals, h, gain.reshape(1, width), sel)
    return (layer_out, draft.reshape(REQ, MAXACC, width))


def solution(mesh):
    return jax.shard_map(
        on_device,
        mesh=mesh,
        in_specs=(
            P("dp", "tensor"),
            P("dp", "tensor", None),
            P("dp", "tensor", None),
            P("dp", None, None),
            P("dp", None, None),
            P("dp", "tensor"),
            P("tensor", None),
            P("tensor"),
            P("dp", None),
            P("dp"),
            P("dp"),
        ),
        out_specs=(P("dp", "tensor"), P("dp", None, "tensor")),
        check_vma=False,
    )
```

```python
import jax
import jax.numpy as jnp
from jax import lax
from jax.experimental import pallas as pl
from jax.experimental.pallas import tpu as pltpu
from jax.sharding import PartitionSpec as P

D = 8192
HD = 128
KVH = 4
TREE = 16
REQ = 4
ROWS = REQ * TREE
MAXACC = 8
HEADS = 32
GROUP = HEADS // KVH
STAT = 8
MSG = ROWS + STAT

floor_score = -1e30
epsilon = 1e-05
score_scale = HD ** (-0.5)
f32 = jnp.float32
bf16 = jnp.bfloat16
VM = pl.BlockSpec(memory_space=pltpu.VMEM)
HB = pl.BlockSpec(memory_space=pltpu.HBM)
SM = pl.BlockSpec(memory_space=pltpu.SMEM)
STAGGER = 10000


def iota(shape, dim):
    return lax.broadcasted_iota(jnp.int32, shape, dim)


def three_parts(x):
    hi = x.astype(bf16).astype(f32)
    mid = (x - hi).astype(bf16).astype(f32)
    return hi, mid, x - hi - mid


def to_all(x):
    return lax.all_to_all(x, "tensor", split_axis=0, concat_axis=0, tiled=True)


def spread_kernel(late, q, out, here, sems):
    fetch = pltpu.make_async_copy(q, here, sems.at[0])
    fetch.start()

    @pl.when(late[0] > 0)
    def _():
        pl.delay(STAGGER)

    fetch.wait()
    copies = [pltpu.make_async_copy(here, out.at[d], sems.at[d]) for d in range(out.shape[0])]
    for copy in copies:
        copy.start()
    for copy in copies:
        copy.wait()


def across(x, groups):
    return lax.all_to_all(
        x, "tensor", split_axis=0, concat_axis=0, axis_index_groups=groups, tiled=True
    )


def tree_kernel(
    rank, parents, acc_node, cache_len, q, kt, vt, k, v, gain,
    o_ref, lse_ref, sel_ref, left_ref, gain_ref,
):
    gain_ref[...] = jnp.broadcast_to(gain[...].astype(f32), gain_ref.shape)
    for r in range(REQ):
        left_ref[r] = jnp.full((8, HD), cache_len[r] - rank[0] * k.shape[1], jnp.int32)
    row = iota((ROWS, ROWS), 0)
    col = iota((ROWS, ROWS), 1)
    same = (row // TREE) == (col // TREE)
    up = jnp.zeros((ROWS, ROWS), jnp.int32)
    for r in range(REQ):
        for i in range(1, TREE):
            up = jnp.where(row == r * TREE + i, parents[r, i] + r * TREE, up)
    link = jnp.where((up == col) & (row % TREE > 0), 1.0, 0.0)
    reach = jnp.where(row == col, 1.0, link)
    for sweep in range((TREE - 1).bit_length()):
        half = reach.astype(bf16)
        reach = jnp.minimum(jnp.dot(half, half, preferred_element_type=f32), 1.0)
    lane = pl.ds(pl.multiple_of((rank[0] // GROUP) * HD, HD), HD)
    keys = jnp.concatenate([kt[r, :, lane] for r in range(REQ)], axis=0)
    values = jnp.concatenate([vt[r, :, lane] for r in range(REQ)], axis=0)
    nt = (((1,), (1,)), ((), ()))
    scores = lax.dot_general(q[...], keys, nt, preferred_element_type=f32) * score_scale
    valid = (reach > 0.5) & same
    scores = jnp.where(valid, scores, floor_score)
    top = jnp.max(scores, axis=1, keepdims=True)
    e = jnp.where(valid, jnp.exp(scores - top), 0.0)
    total = jnp.sum(e, axis=1, keepdims=True)
    o_ref[...] = jnp.dot(e.astype(bf16), values, preferred_element_type=f32) / total
    lse = jnp.broadcast_to(top + jnp.log(total), (ROWS, HD))
    lse_ref[...] = lse.T[:8, :]
    depth = lax.dot_general(
        jnp.ones((8, ROWS), bf16), reach.astype(bf16), nt, preferred_element_type=f32
    )[:1, :] - 1.0
    out = iota((REQ * MAXACC, ROWS), 0)
    lanes = iota((REQ * MAXACC, ROWS), 1)
    chosen = jnp.zeros((REQ * MAXACC, ROWS), jnp.int32)
    for r in range(REQ):
        chosen = jnp.where(out // MAXACC == r, acc_node[r] + r * TREE, chosen)
    onehot = jnp.where(lanes == chosen, 1.0, 0.0).astype(bf16)
    onpath = jnp.dot(onehot, reach.astype(bf16), preferred_element_type=f32)
    level = (out % MAXACC).astype(f32)
    sel_ref[...] = jnp.where(depth == level, onpath, 0.0).astype(bf16)


def attend_kernel(left, q, k, v, out):
    span = k.shape[1]
    nt = (((1,), (1,)), ((), ()))
    tn = (((0,), (0,)), ((), ()))
    pos = iota((span, HD), 0)
    sub = iota((GROUP, HD), 0)
    lane = iota((GROUP, HD), 1)
    packed = [jnp.zeros((GROUP, HD), f32)] * KVH
    for r in range(REQ):
        rows = slice(r * TREE, (r + 1) * TREE)
        valid = pos < left[r, 0:1, :]
        for g in range(KVH):
            cols = slice(g * HD, (g + 1) * HD)
            heads = slice(g * GROUP, (g + 1) * GROUP)
            qh = q[heads, rows, :].reshape(GROUP * TREE, HD)
            s = lax.dot_general(k[r, :, cols], qh, nt, preferred_element_type=f32) * score_scale
            s = jnp.where(valid, s, floor_score)
            top = jnp.max(s, axis=0, keepdims=True)
            e = jnp.where(valid, jnp.exp(s - top), 0.0)
            total = jnp.sum(e, axis=0, keepdims=True)
            some = total > 0.0
            inv = jnp.where(some, 1.0 / jnp.where(some, total, 1.0), 0.0)
            lse = jnp.where(some, top + jnp.log(jnp.where(some, total, 1.0)), floor_score)
            p = (e * inv).astype(bf16)
            o = lax.dot_general(p, v[r, :, cols], tn, preferred_element_type=f32)
            out[heads, rows, :] = o.astype(bf16).reshape(GROUP, TREE, HD)
            turned = pltpu.roll(
                jnp.broadcast_to(pltpu.roll(lse, (r + 1) * TREE, 1), (GROUP, HD)),
                0,
                1,
                stride=TREE,
                stride_axis=0,
            )
            packed[g] = jnp.where(lane // TREE == r, turned, packed[g])
    for g in range(KVH):
        hi, mid, lo = three_parts(packed[g])
        first = jnp.where(lane < ROWS, hi, pltpu.roll(mid, ROWS, 1))
        for j in range(GROUP):
            i = GROUP - 1 - j
            stat = jnp.where(sub == 0, first[i : i + 1, :], jnp.where(sub == 1, lo[i : i + 1, :], 0.0))
            out[g * GROUP + j, ROWS:MSG, :] = stat.astype(bf16)


def project_kernel(got, o_tree, lse_tree, wo, out):
    srcs = got.shape[0]
    stats = got[:, ROWS:MSG, :].astype(f32)
    first = stats[:, 0, :]
    lse = first + pltpu.roll(first, ROWS, 1) + stats[:, 1, :]
    tree = lse_tree[0:1, :]
    tree = jnp.concatenate([tree, jnp.zeros((1, HD - ROWS), f32)], axis=1)
    top = jnp.maximum(jnp.max(lse, axis=0, keepdims=True), tree)
    w = jnp.exp(lse - top)
    wt = jnp.exp(tree - top)
    inv = 1.0 / (jnp.sum(w, axis=0, keepdims=True) + wt)
    every = jnp.concatenate(
        [w * inv, jnp.broadcast_to(wt * inv, (8, HD)), jnp.zeros((HD - srcs - 8, HD), f32)], axis=0
    ).T[:ROWS, :]
    att = o_tree[...] * every[:, srcs : srcs + 1]
    for c in range(srcs):
        att = att + got[c, :ROWS, :].astype(f32) * every[:, c : c + 1]
    att = att.astype(bf16)
    width = out.shape[2]
    for d in range(out.shape[0]):
        part = jnp.dot(att, wo[:, d * width : (d + 1) * width], preferred_element_type=f32)
        out[d] = part.astype(bf16)


def join_kernel(got, out):
    for d in range(out.shape[0]):
        total = got[0, d].astype(f32)
        for c in range(1, got.shape[0]):
            total = total + got[c, d].astype(f32)
        out[d] = total.astype(bf16)


def hidden_kernel(got, residual, h_ref, layer_ref, sq_ref):
    h = residual[...].astype(f32)
    for c in range(got.shape[0]):
        h = h + got[c].astype(f32)
    h_ref[...] = h
    layer_ref[...] = h.astype(bf16)
    sq = h * h
    part = sq[:, :HD]
    for c in range(HD, sq.shape[1], HD):
        part = part + sq[:, c : c + HD]
    row = jnp.sum(part.T, axis=0, keepdims=True)
    row = jnp.concatenate([row, jnp.zeros((1, HD - ROWS), f32)], axis=1)
    hi, mid, lo = three_parts(row)
    sub = iota((STAT, HD), 0)
    tile = jnp.where(sub == 0, hi, jnp.where(sub == 1, mid, jnp.where(sub == 2, lo, 0.0))).astype(bf16)
    for c in range(sq_ref.shape[0]):
        sq_ref[c] = tile


def draft_kernel(got, h, gain, sel, out):
    tile = got[0].astype(f32)
    for c in range(1, got.shape[0]):
        tile = tile + got[c].astype(f32)
    total = jnp.sum(tile, axis=0, keepdims=True)
    scale = lax.rsqrt(jnp.broadcast_to(total / D, (HD, HD)).T[:ROWS, :] + epsilon)
    for c in range(0, h.shape[1], HD):
        cols = slice(c, c + HD)
        feat = (h[:, cols] * scale * gain[0:1, cols]).astype(bf16)
        out[:, cols] = jnp.dot(sel[...], feat, preferred_element_type=f32).astype(bf16)


def params(mib):
    return pltpu.CompilerParams(vmem_limit_bytes=mib * 2**20)


def shape(dims, kind):
    return jax.ShapeDtypeStruct(dims, kind)


def on_device(
    q_rows,
    k_cache,
    v_cache,
    k_tree,
    v_tree,
    residual,
    wo_rows,
    gain,
    parents,
    cache_len,
    accepted_node,
):
    count = lax.axis_size("tensor")
    rank = lax.axis_index("tensor").astype(jnp.int32).reshape(1)
    width = residual.shape[1]
    q_each = pl.pallas_call(
        spread_kernel,
        name="spread",
        compiler_params=params(60),
        out_shape=shape((count, ROWS, HD), bf16),
        in_specs=[SM, HB],
        out_specs=HB,
        scratch_shapes=[pltpu.VMEM((ROWS, HD), bf16), pltpu.SemaphoreType.DMA((count,))],
    )(lax.axis_index("dp").astype(jnp.int32).reshape(1) % 2, q_rows)
    q_all = to_all(q_each)
    o_tree, lse_tree, sel, left, gains = pl.pallas_call(
        tree_kernel,
        name="tree",
        compiler_params=params(6),
        out_shape=(
            shape((ROWS, HD), f32),
            shape((8, ROWS), f32),
            shape((REQ * MAXACC, ROWS), bf16),
            shape((REQ, 8, HD), jnp.int32),
            shape((8, width), f32),
        ),
        in_specs=[SM, SM, SM, SM, VM, VM, VM, VM, VM, VM],
        out_specs=(VM, VM, VM, VM, VM),
        cost_estimate=pl.CostEstimate(flops=10**8, bytes_accessed=4 * 10**6, transcendentals=10000),
    )(
        rank, parents, accepted_node, cache_len, q_rows, k_tree, v_tree, k_cache, v_cache,
        gain.reshape(1, width),
    )
    sent = pl.pallas_call(
        attend_kernel,
        name="attend",
        compiler_params=params(10),
        out_shape=shape((HEADS, MSG, HD), bf16),
        in_specs=[VM, VM, VM, VM],
        out_specs=VM,
    )(left, q_all, k_cache, v_cache)
    got = to_all(sent)
    terms = pl.pallas_call(
        project_kernel,
        name="project",
        compiler_params=params(10),
        out_shape=shape((count, ROWS, width), bf16),
        in_specs=[VM, VM, VM, VM],
        out_specs=VM,
    )(got, o_tree, lse_tree, wo_rows)
    lines, size = 4, count // 4
    along_x = [[x * size + y for x in range(lines)] for y in range(size)]
    along_y = [[x * size + y for y in range(size)] for x in range(lines)]
    part = across(terms.reshape(lines, size * ROWS, width), along_x)
    joined = pl.pallas_call(
        join_kernel,
        name="join",
        compiler_params=params(6),
        out_shape=shape((size, ROWS, width), bf16),
        in_specs=[VM],
        out_specs=VM,
    )(part.reshape(lines, size, ROWS, width))
    arrived = across(joined, along_y)
    h, layer_out, squares = pl.pallas_call(
        hidden_kernel,
        name="hidden",
        compiler_params=params(6),
        out_shape=(shape((ROWS, width), f32), shape((ROWS, width), bf16), shape((count, STAT, HD), bf16)),
        in_specs=[VM, VM],
        out_specs=(VM, VM, VM),
    )(arrived, residual)
    totals = to_all(squares)
    draft = pl.pallas_call(
        draft_kernel,
        name="draft",
        compiler_params=params(4),
        out_shape=shape((REQ * MAXACC, width), bf16),
        in_specs=[VM, VM, VM, VM],
        out_specs=VM,
    )(totals, h, gains, sel)
    return (layer_out, draft.reshape(REQ, MAXACC, width))


def solution(mesh):
    return jax.shard_map(
        on_device,
        mesh=mesh,
        in_specs=(
            P("dp", "tensor"),
            P("dp", "tensor", None),
            P("dp", "tensor", None),
            P("dp", None, None),
            P("dp", None, None),
            P("dp", "tensor"),
            P("tensor", None),
            P("tensor"),
            P("dp", None),
            P("dp"),
            P("dp"),
        ),
        out_specs=(P("dp", "tensor"), P("dp", None, "tensor")),
        check_vma=False,
    )
```

```python
import jax
import jax.numpy as jnp
from jax import lax
from jax.experimental import pallas as pl
from jax.experimental.pallas import tpu as pltpu
from jax.sharding import PartitionSpec as P

D = 8192
HD = 128
KVH = 4
TREE = 16
REQ = 4
ROWS = REQ * TREE
MAXACC = 8
HEADS = 32
GROUP = HEADS // KVH
STAT = 8
MSG = ROWS + STAT

floor_score = -1e30
epsilon = 1e-05
score_scale = HD ** (-0.5)
f32 = jnp.float32
bf16 = jnp.bfloat16
VM = pl.BlockSpec(memory_space=pltpu.VMEM)
SM = pl.BlockSpec(memory_space=pltpu.SMEM)
STAGGER = 9800


def iota(shape, dim):
    return lax.broadcasted_iota(jnp.int32, shape, dim)


def three_parts(x):
    hi = x.astype(bf16).astype(f32)
    mid = (x - hi).astype(bf16).astype(f32)
    return hi, mid, x - hi - mid


def to_all(x):
    return lax.all_to_all(x, "tensor", split_axis=0, concat_axis=0, tiled=True)


def spread_kernel(late, q, out):
    @pl.when(late[0] > 0)
    def _():
        pl.delay(STAGGER)

    for d in range(out.shape[0]):
        out[d] = q[...]


def across(x, groups):
    return lax.all_to_all(
        x, "tensor", split_axis=0, concat_axis=0, axis_index_groups=groups, tiled=True
    )


def tree_kernel(
    rank, parents, acc_node, cache_len, q, kt, vt, k, v, gain,
    o_ref, lse_ref, sel_ref, left_ref, gain_ref,
):
    gain_ref[...] = jnp.broadcast_to(gain[...].astype(f32), gain_ref.shape)
    for r in range(REQ):
        left_ref[r] = jnp.full((8, HD), cache_len[r] - rank[0] * k.shape[1], jnp.int32)
    row = iota((ROWS, ROWS), 0)
    col = iota((ROWS, ROWS), 1)
    same = (row // TREE) == (col // TREE)
    up = jnp.zeros((ROWS, ROWS), jnp.int32)
    for r in range(REQ):
        for i in range(1, TREE):
            up = jnp.where(row == r * TREE + i, parents[r, i] + r * TREE, up)
    link = jnp.where((up == col) & (row % TREE > 0), 1.0, 0.0)
    reach = jnp.where(row == col, 1.0, link)
    for sweep in range((TREE - 1).bit_length()):
        half = reach.astype(bf16)
        reach = jnp.minimum(jnp.dot(half, half, preferred_element_type=f32), 1.0)
    lane = pl.ds(pl.multiple_of((rank[0] // GROUP) * HD, HD), HD)
    keys = jnp.concatenate([kt[r, :, lane] for r in range(REQ)], axis=0)
    values = jnp.concatenate([vt[r, :, lane] for r in range(REQ)], axis=0)
    nt = (((1,), (1,)), ((), ()))
    scores = lax.dot_general(q[...], keys, nt, preferred_element_type=f32) * score_scale
    valid = (reach > 0.5) & same
    scores = jnp.where(valid, scores, floor_score)
    top = jnp.max(scores, axis=1, keepdims=True)
    e = jnp.where(valid, jnp.exp(scores - top), 0.0)
    total = jnp.sum(e, axis=1, keepdims=True)
    o_ref[...] = jnp.dot(e.astype(bf16), values, preferred_element_type=f32) / total
    lse = jnp.broadcast_to(top + jnp.log(total), (ROWS, HD))
    lse_ref[...] = lse.T[:8, :]
    depth = lax.dot_general(
        jnp.ones((8, ROWS), bf16), reach.astype(bf16), nt, preferred_element_type=f32
    )[:1, :] - 1.0
    out = iota((REQ * MAXACC, ROWS), 0)
    lanes = iota((REQ * MAXACC, ROWS), 1)
    chosen = jnp.zeros((REQ * MAXACC, ROWS), jnp.int32)
    for r in range(REQ):
        chosen = jnp.where(out // MAXACC == r, acc_node[r] + r * TREE, chosen)
    onehot = jnp.where(lanes == chosen, 1.0, 0.0).astype(bf16)
    onpath = jnp.dot(onehot, reach.astype(bf16), preferred_element_type=f32)
    level = (out % MAXACC).astype(f32)
    sel_ref[...] = jnp.where(depth == level, onpath, 0.0).astype(bf16)


def attend_kernel(left, q, k, v, out):
    span = k.shape[1]
    nt = (((1,), (1,)), ((), ()))
    tn = (((0,), (0,)), ((), ()))
    pos = iota((span, HD), 0)
    sub = iota((GROUP, HD), 0)
    lane = iota((GROUP, HD), 1)
    packed = [jnp.zeros((GROUP, HD), f32)] * KVH
    for r in range(REQ):
        rows = slice(r * TREE, (r + 1) * TREE)
        valid = pos < left[r, 0:1, :]
        for g in range(KVH):
            cols = slice(g * HD, (g + 1) * HD)
            heads = slice(g * GROUP, (g + 1) * GROUP)
            qh = q[heads, rows, :].reshape(GROUP * TREE, HD)
            s = lax.dot_general(k[r, :, cols], qh, nt, preferred_element_type=f32) * score_scale
            s = jnp.where(valid, s, floor_score)
            top = jnp.max(s, axis=0, keepdims=True)
            e = jnp.exp(s - top)
            total = jnp.sum(e, axis=0, keepdims=True)
            some = left[r, 0:1, :] > 0
            inv = jnp.where(some, 1.0 / total, 0.0)
            lse = jnp.where(some, top + jnp.log(total), floor_score)
            p = (e * inv).astype(bf16)
            o = lax.dot_general(p, v[r, :, cols], tn, preferred_element_type=f32)
            out[heads, rows, :] = o.astype(bf16).reshape(GROUP, TREE, HD)
            turned = pltpu.roll(
                jnp.broadcast_to(pltpu.roll(lse, (r + 1) * TREE, 1), (GROUP, HD)),
                0,
                1,
                stride=TREE,
                stride_axis=0,
            )
            packed[g] = jnp.where(lane // TREE == r, turned, packed[g])
    for g in range(KVH):
        hi, mid, lo = three_parts(packed[g])
        first = jnp.where(lane < ROWS, hi, pltpu.roll(mid, ROWS, 1))
        for j in range(GROUP):
            i = GROUP - 1 - j
            stat = jnp.where(sub == 0, first[i : i + 1, :], jnp.where(sub == 1, lo[i : i + 1, :], 0.0))
            out[g * GROUP + j, ROWS:MSG, :] = stat.astype(bf16)


def project_kernel(got, o_tree, lse_tree, wo, out):
    srcs = got.shape[0]
    stats = got[:, ROWS:MSG, :].astype(f32)
    first = stats[:, 0, :]
    lse = first + pltpu.roll(first, ROWS, 1) + stats[:, 1, :]
    tree = lse_tree[0:1, :]
    tree = jnp.concatenate([tree, jnp.zeros((1, HD - ROWS), f32)], axis=1)
    top = jnp.maximum(jnp.max(lse, axis=0, keepdims=True), tree)
    w = jnp.exp(lse - top)
    wt = jnp.exp(tree - top)
    inv = 1.0 / (jnp.sum(w, axis=0, keepdims=True) + wt)
    every = jnp.concatenate(
        [w * inv, jnp.broadcast_to(wt * inv, (8, HD)), jnp.zeros((HD - srcs - 8, HD), f32)], axis=0
    ).T[:ROWS, :]
    att = o_tree[...] * every[:, srcs : srcs + 1]
    for c in range(srcs):
        att = att + got[c, :ROWS, :].astype(f32) * every[:, c : c + 1]
    att = att.astype(bf16)
    width = out.shape[2]
    for d in range(out.shape[0]):
        part = jnp.dot(att, wo[:, d * width : (d + 1) * width], preferred_element_type=f32)
        out[d] = part.astype(bf16)


def join_kernel(got, out):
    for d in range(out.shape[0]):
        total = got[0, d].astype(f32)
        for c in range(1, got.shape[0]):
            total = total + got[c, d].astype(f32)
        out[d] = total.astype(bf16)


def hidden_kernel(got, residual, h_ref, layer_ref, sq_ref):
    h = residual[...].astype(f32)
    for c in range(got.shape[0]):
        h = h + got[c].astype(f32)
    h_ref[...] = h
    layer_ref[...] = h.astype(bf16)
    sq = h * h
    part = sq[:, :HD]
    for c in range(HD, sq.shape[1], HD):
        part = part + sq[:, c : c + HD]
    row = jnp.sum(part.T, axis=0, keepdims=True)
    row = jnp.concatenate([row, jnp.zeros((1, HD - ROWS), f32)], axis=1)
    hi, mid, lo = three_parts(row)
    sub = iota((STAT, HD), 0)
    tile = jnp.where(sub == 0, hi, jnp.where(sub == 1, mid, jnp.where(sub == 2, lo, 0.0))).astype(bf16)
    for c in range(sq_ref.shape[0]):
        sq_ref[c] = tile


def draft_kernel(got, h, gain, sel, out):
    tile = got[0].astype(f32)
    for c in range(1, got.shape[0]):
        tile = tile + got[c].astype(f32)
    total = jnp.sum(tile, axis=0, keepdims=True)
    scale = lax.rsqrt(jnp.broadcast_to(total / D, (HD, HD)).T[:ROWS, :] + epsilon)
    for c in range(0, h.shape[1], HD):
        cols = slice(c, c + HD)
        feat = (h[:, cols] * scale * gain[0:1, cols]).astype(bf16)
        out[:, cols] = jnp.dot(sel[...], feat, preferred_element_type=f32).astype(bf16)


def params(mib):
    return pltpu.CompilerParams(vmem_limit_bytes=mib * 2**20)


def shape(dims, kind):
    return jax.ShapeDtypeStruct(dims, kind)


def on_device(
    q_rows,
    k_cache,
    v_cache,
    k_tree,
    v_tree,
    residual,
    wo_rows,
    gain,
    parents,
    cache_len,
    accepted_node,
):
    count = lax.axis_size("tensor")
    rank = lax.axis_index("tensor").astype(jnp.int32).reshape(1)
    width = residual.shape[1]
    q_each = pl.pallas_call(
        spread_kernel,
        name="spread",
        compiler_params=params(2),
        out_shape=shape((count, ROWS, HD), bf16),
        in_specs=[SM, VM],
        out_specs=VM,
    )(lax.axis_index("dp").astype(jnp.int32).reshape(1) % 2, q_rows)
    q_all = to_all(q_each)
    o_tree, lse_tree, sel, left, gains = pl.pallas_call(
        tree_kernel,
        name="tree",
        compiler_params=params(6),
        out_shape=(
            shape((ROWS, HD), f32),
            shape((8, ROWS), f32),
            shape((REQ * MAXACC, ROWS), bf16),
            shape((REQ, 8, HD), jnp.int32),
            shape((8, width), f32),
        ),
        in_specs=[SM, SM, SM, SM, VM, VM, VM, VM, VM, VM],
        out_specs=(VM, VM, VM, VM, VM),
        cost_estimate=pl.CostEstimate(flops=10**8, bytes_accessed=4 * 10**6, transcendentals=10000),
    )(
        rank, parents, accepted_node, cache_len, q_rows, k_tree, v_tree, k_cache, v_cache,
        gain.reshape(1, width),
    )
    sent = pl.pallas_call(
        attend_kernel,
        name="attend",
        compiler_params=params(10),
        out_shape=shape((HEADS, MSG, HD), bf16),
        in_specs=[VM, VM, VM, VM],
        out_specs=VM,
    )(left, q_all, k_cache, v_cache)
    got = to_all(sent)
    terms = pl.pallas_call(
        project_kernel,
        name="project",
        compiler_params=params(10),
        out_shape=shape((count, ROWS, width), bf16),
        in_specs=[VM, VM, VM, VM],
        out_specs=VM,
    )(got, o_tree, lse_tree, wo_rows)
    lines, size = 4, count // 4
    along_x = [[x * size + y for x in range(lines)] for y in range(size)]
    along_y = [[x * size + y for y in range(size)] for x in range(lines)]
    part = across(terms.reshape(lines, size * ROWS, width), along_x)
    joined = pl.pallas_call(
        join_kernel,
        name="join",
        compiler_params=params(6),
        out_shape=shape((size, ROWS, width), bf16),
        in_specs=[VM],
        out_specs=VM,
    )(part.reshape(lines, size, ROWS, width))
    arrived = across(joined, along_y)
    h, layer_out, squares = pl.pallas_call(
        hidden_kernel,
        name="hidden",
        compiler_params=params(6),
        out_shape=(shape((ROWS, width), f32), shape((ROWS, width), bf16), shape((count, STAT, HD), bf16)),
        in_specs=[VM, VM],
        out_specs=(VM, VM, VM),
    )(arrived, residual)
    totals = to_all(squares)
    draft = pl.pallas_call(
        draft_kernel,
        name="draft",
        compiler_params=params(4),
        out_shape=shape((REQ * MAXACC, width), bf16),
        in_specs=[VM, VM, VM, VM],
        out_specs=VM,
    )(totals, h, gains, sel)
    return (layer_out, draft.reshape(REQ, MAXACC, width))


def solution(mesh):
    return jax.shard_map(
        on_device,
        mesh=mesh,
        in_specs=(
            P("dp", "tensor"),
            P("dp", "tensor", None),
            P("dp", "tensor", None),
            P("dp", None, None),
            P("dp", None, None),
            P("dp", "tensor"),
            P("tensor", None),
            P("tensor"),
            P("dp", None),
            P("dp"),
            P("dp"),
        ),
        out_specs=(P("dp", "tensor"), P("dp", None, "tensor")),
        check_vma=False,
    )
```

```python
import jax
import jax.numpy as jnp
from jax import lax
from jax.experimental import pallas as pl
from jax.experimental.pallas import tpu as pltpu
from jax.sharding import PartitionSpec as P

D = 8192
HD = 128
KVH = 4
TREE = 16
REQ = 4
ROWS = REQ * TREE
MAXACC = 8
HEADS = 32
GROUP = HEADS // KVH
STAT = 8
MSG = ROWS + STAT

floor_score = -1e30
epsilon = 1e-05
score_scale = HD ** (-0.5)
f32 = jnp.float32
bf16 = jnp.bfloat16
VM = pl.BlockSpec(memory_space=pltpu.VMEM)
SM = pl.BlockSpec(memory_space=pltpu.SMEM)
STAGGER = 9400


def iota(shape, dim):
    return lax.broadcasted_iota(jnp.int32, shape, dim)


def three_parts(x):
    hi = x.astype(bf16).astype(f32)
    mid = (x - hi).astype(bf16).astype(f32)
    return hi, mid, x - hi - mid


def to_all(x):
    return lax.all_to_all(x, "tensor", split_axis=0, concat_axis=0, tiled=True)


def spread_kernel(late, q, out):
    @pl.when(late[0] > 0)
    def _():
        pl.delay(STAGGER)

    for d in range(out.shape[0]):
        out[d] = q[...]


def across(x, groups):
    return lax.all_to_all(
        x, "tensor", split_axis=0, concat_axis=0, axis_index_groups=groups, tiled=True
    )


def tree_kernel(
    rank, parents, acc_node, cache_len, q, kt, vt, k, v, gain,
    o_ref, lse_ref, sel_ref, left_ref, gain_ref,
):
    gain_ref[...] = jnp.broadcast_to(gain[...].astype(f32), gain_ref.shape)
    for r in range(REQ):
        left_ref[r] = jnp.full((8, HD), cache_len[r] - rank[0] * k.shape[1], jnp.int32)
    row = iota((ROWS, ROWS), 0)
    col = iota((ROWS, ROWS), 1)
    same = (row // TREE) == (col // TREE)
    up = jnp.zeros((ROWS, ROWS), jnp.int32)
    for r in range(REQ):
        for i in range(1, TREE):
            up = jnp.where(row == r * TREE + i, parents[r, i] + r * TREE, up)
    link = jnp.where((up == col) & (row % TREE > 0), 1.0, 0.0)
    reach = jnp.where(row == col, 1.0, link)
    for sweep in range((TREE - 1).bit_length()):
        half = reach.astype(bf16)
        reach = jnp.minimum(jnp.dot(half, half, preferred_element_type=f32), 1.0)
    lane = pl.ds(pl.multiple_of((rank[0] // GROUP) * HD, HD), HD)
    keys = jnp.concatenate([kt[r, :, lane] for r in range(REQ)], axis=0)
    values = jnp.concatenate([vt[r, :, lane] for r in range(REQ)], axis=0)
    nt = (((1,), (1,)), ((), ()))
    scores = lax.dot_general(q[...], keys, nt, preferred_element_type=f32) * score_scale
    valid = (reach > 0.5) & same
    scores = jnp.where(valid, scores, floor_score)
    top = jnp.max(scores, axis=1, keepdims=True)
    e = jnp.where(valid, jnp.exp(scores - top), 0.0)
    total = jnp.sum(e, axis=1, keepdims=True)
    o_ref[...] = jnp.dot(e.astype(bf16), values, preferred_element_type=f32) / total
    lse = jnp.broadcast_to(top + jnp.log(total), (ROWS, HD))
    lse_ref[...] = lse.T[:8, :]
    depth = lax.dot_general(
        jnp.ones((8, ROWS), bf16), reach.astype(bf16), nt, preferred_element_type=f32
    )[:1, :] - 1.0
    out = iota((REQ * MAXACC, ROWS), 0)
    lanes = iota((REQ * MAXACC, ROWS), 1)
    chosen = jnp.zeros((REQ * MAXACC, ROWS), jnp.int32)
    for r in range(REQ):
        chosen = jnp.where(out // MAXACC == r, acc_node[r] + r * TREE, chosen)
    onehot = jnp.where(lanes == chosen, 1.0, 0.0).astype(bf16)
    onpath = jnp.dot(onehot, reach.astype(bf16), preferred_element_type=f32)
    level = (out % MAXACC).astype(f32)
    sel_ref[...] = jnp.where(depth == level, onpath, 0.0).astype(bf16)


def attend_kernel(left, q, k, v, out):
    span = k.shape[1]
    nt = (((1,), (1,)), ((), ()))
    tn = (((0,), (0,)), ((), ()))
    pos = iota((span, HD), 0)
    sub = iota((GROUP, HD), 0)
    lane = iota((GROUP, HD), 1)
    packed = [jnp.zeros((GROUP, HD), f32)] * KVH
    for r in range(REQ):
        rows = slice(r * TREE, (r + 1) * TREE)
        valid = pos < left[r, 0:1, :]
        for g in range(KVH):
            cols = slice(g * HD, (g + 1) * HD)
            heads = slice(g * GROUP, (g + 1) * GROUP)
            qh = q[heads, rows, :].reshape(GROUP * TREE, HD)
            s = lax.dot_general(k[r, :, cols], qh, nt, preferred_element_type=f32) * score_scale
            s = jnp.where(valid, s, floor_score)
            top = jnp.max(s, axis=0, keepdims=True)
            e = jnp.exp(s - top)
            total = jnp.sum(e, axis=0, keepdims=True)
            some = left[r, 0:1, :] > 0
            inv = jnp.where(some, 1.0 / total, 0.0)
            lse = jnp.where(some, top + jnp.log(total), floor_score)
            p = (e * inv).astype(bf16)
            o = lax.dot_general(p, v[r, :, cols], tn, preferred_element_type=f32)
            out[heads, rows, :] = o.astype(bf16).reshape(GROUP, TREE, HD)
            turned = pltpu.roll(
                jnp.broadcast_to(pltpu.roll(lse, (r + 1) * TREE, 1), (GROUP, HD)),
                0,
                1,
                stride=TREE,
                stride_axis=0,
            )
            packed[g] = jnp.where(lane // TREE == r, turned, packed[g])
    for g in range(KVH):
        hi, mid, lo = three_parts(packed[g])
        first = jnp.where(lane < ROWS, hi, pltpu.roll(mid, ROWS, 1))
        for j in range(GROUP):
            i = GROUP - 1 - j
            stat = jnp.where(sub == 0, first[i : i + 1, :], jnp.where(sub == 1, lo[i : i + 1, :], 0.0))
            out[g * GROUP + j, ROWS:MSG, :] = stat.astype(bf16)


def project_kernel(got, o_tree, lse_tree, wo, out):
    srcs = got.shape[0]
    stats = got[:, ROWS:MSG, :].astype(f32)
    first = stats[:, 0, :]
    lse = first + pltpu.roll(first, ROWS, 1) + stats[:, 1, :]
    tree = lse_tree[0:1, :]
    tree = jnp.concatenate([tree, jnp.zeros((1, HD - ROWS), f32)], axis=1)
    top = jnp.maximum(jnp.max(lse, axis=0, keepdims=True), tree)
    w = jnp.exp(lse - top)
    wt = jnp.exp(tree - top)
    inv = 1.0 / (jnp.sum(w, axis=0, keepdims=True) + wt)
    every = jnp.concatenate(
        [w * inv, jnp.broadcast_to(wt * inv, (8, HD)), jnp.zeros((HD - srcs - 8, HD), f32)], axis=0
    ).T[:ROWS, :]
    att = o_tree[...] * every[:, srcs : srcs + 1]
    for c in range(srcs):
        att = att + got[c, :ROWS, :].astype(f32) * every[:, c : c + 1]
    att = att.astype(bf16)
    width = out.shape[2]
    for d in range(out.shape[0]):
        part = jnp.dot(att, wo[:, d * width : (d + 1) * width], preferred_element_type=f32)
        x, y = d // 8, d % 8
        out[x * 8 + (y % 2) * 4 + y // 2] = part.astype(bf16)


def join_kernel(got, out):
    for d in range(out.shape[0]):
        total = got[0, d].astype(f32)
        for c in range(1, got.shape[0]):
            total = total + got[c, d].astype(f32)
        out[d] = total.astype(bf16)


def hidden_kernel(got, residual, h_ref, layer_ref, sq_ref):
    h = residual[...].astype(f32)
    for c in range(got.shape[0]):
        h = h + got[c].astype(f32)
    h_ref[...] = h
    layer_ref[...] = h.astype(bf16)
    sq = h * h
    part = sq[:, :HD]
    for c in range(HD, sq.shape[1], HD):
        part = part + sq[:, c : c + HD]
    row = jnp.sum(part.T, axis=0, keepdims=True)
    row = jnp.concatenate([row, jnp.zeros((1, HD - ROWS), f32)], axis=1)
    hi, mid, lo = three_parts(row)
    sub = iota((STAT, HD), 0)
    tile = jnp.where(sub == 0, hi, jnp.where(sub == 1, mid, jnp.where(sub == 2, lo, 0.0))).astype(bf16)
    for c in range(sq_ref.shape[0]):
        sq_ref[c] = tile


def draft_kernel(got, h, gain, sel, out):
    tile = got[0].astype(f32)
    for c in range(1, got.shape[0]):
        tile = tile + got[c].astype(f32)
    total = jnp.sum(tile, axis=0, keepdims=True)
    scale = lax.rsqrt(jnp.broadcast_to(total / D, (HD, HD)).T[:ROWS, :] + epsilon)
    for c in range(0, h.shape[1], HD):
        cols = slice(c, c + HD)
        feat = (h[:, cols] * scale * gain[0:1, cols]).astype(bf16)
        out[:, cols] = jnp.dot(sel[...], feat, preferred_element_type=f32).astype(bf16)


def params(mib):
    return pltpu.CompilerParams(vmem_limit_bytes=mib * 2**20)


def shape(dims, kind):
    return jax.ShapeDtypeStruct(dims, kind)


def on_device(
    q_rows,
    k_cache,
    v_cache,
    k_tree,
    v_tree,
    residual,
    wo_rows,
    gain,
    parents,
    cache_len,
    accepted_node,
):
    count = lax.axis_size("tensor")
    rank = lax.axis_index("tensor").astype(jnp.int32).reshape(1)
    width = residual.shape[1]
    q_each = pl.pallas_call(
        spread_kernel,
        name="spread",
        compiler_params=params(2),
        out_shape=shape((count, ROWS, HD), bf16),
        in_specs=[SM, VM],
        out_specs=VM,
    )(lax.axis_index("dp").astype(jnp.int32).reshape(1) % 2, q_rows)
    q_all = to_all(q_each)
    o_tree, lse_tree, sel, left, gains = pl.pallas_call(
        tree_kernel,
        name="tree",
        compiler_params=params(6),
        out_shape=(
            shape((ROWS, HD), f32),
            shape((8, ROWS), f32),
            shape((REQ * MAXACC, ROWS), bf16),
            shape((REQ, 8, HD), jnp.int32),
            shape((8, width), f32),
        ),
        in_specs=[SM, SM, SM, SM, VM, VM, VM, VM, VM, VM],
        out_specs=(VM, VM, VM, VM, VM),
        cost_estimate=pl.CostEstimate(flops=10**8, bytes_accessed=4 * 10**6, transcendentals=10000),
    )(
        rank, parents, accepted_node, cache_len, q_rows, k_tree, v_tree, k_cache, v_cache,
        gain.reshape(1, width),
    )
    sent = pl.pallas_call(
        attend_kernel,
        name="attend",
        compiler_params=params(10),
        out_shape=shape((HEADS, MSG, HD), bf16),
        in_specs=[VM, VM, VM, VM],
        out_specs=VM,
    )(left, q_all, k_cache, v_cache)
    got = to_all(sent)
    terms = pl.pallas_call(
        project_kernel,
        name="project",
        compiler_params=params(10),
        out_shape=shape((count, ROWS, width), bf16),
        in_specs=[VM, VM, VM, VM],
        out_specs=VM,
    )(got, o_tree, lse_tree, wo_rows)
    blocks = [[x * 8 + 2 * b + a for x in range(4) for a in range(2)] for b in range(4)]
    strides = [[x * 8 + 2 * b + a for b in range(4)] for x in range(4) for a in range(2)]
    part = across(terms.reshape(8, 4 * ROWS, width), blocks)
    joined = pl.pallas_call(
        join_kernel,
        name="join",
        compiler_params=params(6),
        out_shape=shape((4, ROWS, width), bf16),
        in_specs=[VM],
        out_specs=VM,
    )(part.reshape(8, 4, ROWS, width))
    arrived = across(joined, strides)
    h, layer_out, squares = pl.pallas_call(
        hidden_kernel,
        name="hidden",
        compiler_params=params(6),
        out_shape=(shape((ROWS, width), f32), shape((ROWS, width), bf16), shape((count, STAT, HD), bf16)),
        in_specs=[VM, VM],
        out_specs=(VM, VM, VM),
    )(arrived, residual)
    totals = to_all(squares)
    draft = pl.pallas_call(
        draft_kernel,
        name="draft",
        compiler_params=params(4),
        out_shape=shape((REQ * MAXACC, width), bf16),
        in_specs=[VM, VM, VM, VM],
        out_specs=VM,
    )(totals, h, gains, sel)
    return (layer_out, draft.reshape(REQ, MAXACC, width))


def solution(mesh):
    return jax.shard_map(
        on_device,
        mesh=mesh,
        in_specs=(
            P("dp", "tensor"),
            P("dp", "tensor", None),
            P("dp", "tensor", None),
            P("dp", None, None),
            P("dp", None, None),
            P("dp", "tensor"),
            P("tensor", None),
            P("tensor"),
            P("dp", None),
            P("dp"),
            P("dp"),
        ),
        out_specs=(P("dp", "tensor"), P("dp", None, "tensor")),
        check_vma=False,
    )
```

```python
import jax
import jax.numpy as jnp
from jax import lax
from jax.experimental import pallas as pl
from jax.experimental.pallas import tpu as pltpu
from jax.sharding import PartitionSpec as P

D = 8192
HD = 128
KVH = 4
TREE = 16
REQ = 4
ROWS = REQ * TREE
MAXACC = 8
HEADS = 32
GROUP = HEADS // KVH
STAT = 8
MSG = ROWS + STAT

floor_score = -1e30
epsilon = 1e-05
score_scale = HD ** (-0.5)
f32 = jnp.float32
bf16 = jnp.bfloat16
VM = pl.BlockSpec(memory_space=pltpu.VMEM)
SM = pl.BlockSpec(memory_space=pltpu.SMEM)
STAGGER = 9600


def iota(shape, dim):
    return lax.broadcasted_iota(jnp.int32, shape, dim)


def three_parts(x):
    hi = x.astype(bf16).astype(f32)
    mid = (x - hi).astype(bf16).astype(f32)
    return hi, mid, x - hi - mid


def to_all(x):
    return lax.all_to_all(x, "tensor", split_axis=0, concat_axis=0, tiled=True)


def spread_kernel(late, q, out):
    @pl.when(late[0] > 0)
    def _():
        pl.delay(STAGGER)

    for d in range(out.shape[0]):
        out[d] = q[...]


def across(x, groups):
    return lax.all_to_all(
        x, "tensor", split_axis=0, concat_axis=0, axis_index_groups=groups, tiled=True
    )


def tree_kernel(
    rank, parents, acc_node, cache_len, q, kt, vt, k, v, gain,
    o_ref, lse_ref, sel_ref, left_ref, gain_ref,
):
    gain_ref[...] = jnp.broadcast_to(gain[...].astype(f32), gain_ref.shape)
    for r in range(REQ):
        left_ref[r] = jnp.full((8, HD), cache_len[r] - rank[0] * k.shape[1], jnp.int32)
    row = iota((ROWS, ROWS), 0)
    col = iota((ROWS, ROWS), 1)
    same = (row // TREE) == (col // TREE)
    up = jnp.zeros((ROWS, ROWS), jnp.int32)
    for r in range(REQ):
        for i in range(1, TREE):
            up = jnp.where(row == r * TREE + i, parents[r, i] + r * TREE, up)
    link = jnp.where((up == col) & (row % TREE > 0), 1.0, 0.0)
    reach = jnp.where(row == col, 1.0, link)
    for sweep in range((TREE - 1).bit_length()):
        half = reach.astype(bf16)
        reach = jnp.minimum(jnp.dot(half, half, preferred_element_type=f32), 1.0)
    lane = pl.ds(pl.multiple_of((rank[0] // GROUP) * HD, HD), HD)
    keys = jnp.concatenate([kt[r, :, lane] for r in range(REQ)], axis=0)
    values = jnp.concatenate([vt[r, :, lane] for r in range(REQ)], axis=0)
    nt = (((1,), (1,)), ((), ()))
    scores = lax.dot_general(q[...], keys, nt, preferred_element_type=f32) * score_scale
    valid = (reach > 0.5) & same
    scores = jnp.where(valid, scores, floor_score)
    top = jnp.max(scores, axis=1, keepdims=True)
    e = jnp.where(valid, jnp.exp(scores - top), 0.0)
    total = jnp.sum(e, axis=1, keepdims=True)
    o_ref[...] = jnp.dot(e.astype(bf16), values, preferred_element_type=f32) / total
    lse = jnp.broadcast_to(top + jnp.log(total), (ROWS, HD))
    lse_ref[...] = lse.T[:8, :]
    depth = lax.dot_general(
        jnp.ones((8, ROWS), bf16), reach.astype(bf16), nt, preferred_element_type=f32
    )[:1, :] - 1.0
    out = iota((REQ * MAXACC, ROWS), 0)
    lanes = iota((REQ * MAXACC, ROWS), 1)
    chosen = jnp.zeros((REQ * MAXACC, ROWS), jnp.int32)
    for r in range(REQ):
        chosen = jnp.where(out // MAXACC == r, acc_node[r] + r * TREE, chosen)
    onehot = jnp.where(lanes == chosen, 1.0, 0.0).astype(bf16)
    onpath = jnp.dot(onehot, reach.astype(bf16), preferred_element_type=f32)
    level = (out % MAXACC).astype(f32)
    sel_ref[...] = jnp.where(depth == level, onpath, 0.0).astype(bf16)


def attend_kernel(left, q, k, v, out):
    span = k.shape[1]
    nt = (((1,), (1,)), ((), ()))
    tn = (((0,), (0,)), ((), ()))
    pos = iota((span, HD), 0)
    sub = iota((GROUP, HD), 0)
    lane = iota((GROUP, HD), 1)
    packed = [jnp.zeros((GROUP, HD), f32)] * KVH
    for r in range(REQ):
        rows = slice(r * TREE, (r + 1) * TREE)
        valid = pos < left[r, 0:1, :]
        for g in range(KVH):
            cols = slice(g * HD, (g + 1) * HD)
            heads = slice(g * GROUP, (g + 1) * GROUP)
            qh = q[heads, rows, :].reshape(GROUP * TREE, HD)
            s = lax.dot_general(k[r, :, cols], qh, nt, preferred_element_type=f32) * score_scale
            s = jnp.where(valid, s, floor_score)
            top = jnp.max(s, axis=0, keepdims=True)
            e = jnp.exp(s - top)
            total = jnp.sum(e, axis=0, keepdims=True)
            some = left[r, 0:1, :] > 0
            inv = jnp.where(some, 1.0 / total, 0.0)
            lse = jnp.where(some, top + jnp.log(total), floor_score)
            p = (e * inv).astype(bf16)
            o = lax.dot_general(p, v[r, :, cols], tn, preferred_element_type=f32)
            out[heads, rows, :] = o.astype(bf16).reshape(GROUP, TREE, HD)
            turned = pltpu.roll(
                jnp.broadcast_to(pltpu.roll(lse, (r + 1) * TREE, 1), (GROUP, HD)),
                0,
                1,
                stride=TREE,
                stride_axis=0,
            )
            packed[g] = jnp.where(lane // TREE == r, turned, packed[g])
    for g in range(KVH):
        hi, mid, lo = three_parts(packed[g])
        first = jnp.where(lane < ROWS, hi, pltpu.roll(mid, ROWS, 1))
        for j in range(GROUP):
            i = GROUP - 1 - j
            stat = jnp.where(sub == 0, first[i : i + 1, :], jnp.where(sub == 1, lo[i : i + 1, :], 0.0))
            out[g * GROUP + j, ROWS:MSG, :] = stat.astype(bf16)


def project_kernel(got, o_tree, lse_tree, wo, out):
    srcs = got.shape[0]
    stats = got[:, ROWS:MSG, :].astype(f32)
    first = stats[:, 0, :]
    lse = first + pltpu.roll(first, ROWS, 1) + stats[:, 1, :]
    tree = lse_tree[0:1, :]
    tree = jnp.concatenate([tree, jnp.zeros((1, HD - ROWS), f32)], axis=1)
    top = jnp.maximum(jnp.max(lse, axis=0, keepdims=True), tree)
    w = jnp.exp(lse - top)
    wt = jnp.exp(tree - top)
    inv = 1.0 / (jnp.sum(w, axis=0, keepdims=True) + wt)
    every = jnp.concatenate(
        [w * inv, jnp.broadcast_to(wt * inv, (8, HD)), jnp.zeros((HD - srcs - 8, HD), f32)], axis=0
    ).T[:ROWS, :]
    att = o_tree[...] * every[:, srcs : srcs + 1]
    for c in range(srcs):
        att = att + got[c, :ROWS, :].astype(f32) * every[:, c : c + 1]
    att = att.astype(bf16)
    width = out.shape[2]
    for d in range(out.shape[0]):
        part = jnp.dot(att, wo[:, d * width : (d + 1) * width], preferred_element_type=f32)
        x, y = d // 8, d % 8
        out[x * 8 + (y % 2) * 4 + y // 2] = part.astype(bf16)


def join_kernel(got, out):
    for d in range(out.shape[0]):
        total = got[0, d].astype(f32)
        for c in range(1, got.shape[0]):
            total = total + got[c, d].astype(f32)
        out[d] = total.astype(bf16)


def hidden_kernel(got, residual, h_ref, sq_ref):
    h = residual[...].astype(f32)
    for c in range(got.shape[0]):
        h = h + got[c].astype(f32)
    h_ref[...] = h
    sq = h * h
    part = sq[:, :HD]
    for c in range(HD, sq.shape[1], HD):
        part = part + sq[:, c : c + HD]
    row = jnp.sum(part.T, axis=0, keepdims=True)
    row = jnp.concatenate([row, jnp.zeros((1, HD - ROWS), f32)], axis=1)
    hi, mid, lo = three_parts(row)
    sub = iota((STAT, HD), 0)
    tile = jnp.where(sub == 0, hi, jnp.where(sub == 1, mid, jnp.where(sub == 2, lo, 0.0))).astype(bf16)
    for c in range(sq_ref.shape[0]):
        sq_ref[c] = tile


def draft_kernel(got, h, gain, sel, out, layer_ref):
    layer_ref[...] = h[...].astype(bf16)
    tile = got[0].astype(f32)
    for c in range(1, got.shape[0]):
        tile = tile + got[c].astype(f32)
    total = jnp.sum(tile, axis=0, keepdims=True)
    scale = lax.rsqrt(jnp.broadcast_to(total / D, (HD, HD)).T[:ROWS, :] + epsilon)
    for c in range(0, h.shape[1], HD):
        cols = slice(c, c + HD)
        feat = (h[:, cols] * scale * gain[0:1, cols]).astype(bf16)
        out[:, cols] = jnp.dot(sel[...], feat, preferred_element_type=f32).astype(bf16)


def params(mib):
    return pltpu.CompilerParams(vmem_limit_bytes=mib * 2**20)


def shape(dims, kind):
    return jax.ShapeDtypeStruct(dims, kind)


def on_device(
    q_rows,
    k_cache,
    v_cache,
    k_tree,
    v_tree,
    residual,
    wo_rows,
    gain,
    parents,
    cache_len,
    accepted_node,
):
    count = lax.axis_size("tensor")
    rank = lax.axis_index("tensor").astype(jnp.int32).reshape(1)
    width = residual.shape[1]
    q_each = pl.pallas_call(
        spread_kernel,
        name="spread",
        compiler_params=params(2),
        out_shape=shape((count, ROWS, HD), bf16),
        in_specs=[SM, VM],
        out_specs=VM,
    )(lax.axis_index("dp").astype(jnp.int32).reshape(1) % 2, q_rows)
    q_all = to_all(q_each)
    o_tree, lse_tree, sel, left, gains = pl.pallas_call(
        tree_kernel,
        name="tree",
        compiler_params=params(6),
        out_shape=(
            shape((ROWS, HD), f32),
            shape((8, ROWS), f32),
            shape((REQ * MAXACC, ROWS), bf16),
            shape((REQ, 8, HD), jnp.int32),
            shape((8, width), f32),
        ),
        in_specs=[SM, SM, SM, SM, VM, VM, VM, VM, VM, VM],
        out_specs=(VM, VM, VM, VM, VM),
        cost_estimate=pl.CostEstimate(flops=10**8, bytes_accessed=4 * 10**6, transcendentals=10000),
    )(
        rank, parents, accepted_node, cache_len, q_rows, k_tree, v_tree, k_cache, v_cache,
        gain.reshape(1, width),
    )
    sent = pl.pallas_call(
        attend_kernel,
        name="attend",
        compiler_params=params(10),
        out_shape=shape((HEADS, MSG, HD), bf16),
        in_specs=[VM, VM, VM, VM],
        out_specs=VM,
    )(left, q_all, k_cache, v_cache)
    got = to_all(sent)
    terms = pl.pallas_call(
        project_kernel,
        name="project",
        compiler_params=params(10),
        out_shape=shape((count, ROWS, width), bf16),
        in_specs=[VM, VM, VM, VM],
        out_specs=VM,
    )(got, o_tree, lse_tree, wo_rows)
    blocks = [[x * 8 + 2 * b + a for x in range(4) for a in range(2)] for b in range(4)]
    strides = [[x * 8 + 2 * b + a for b in range(4)] for x in range(4) for a in range(2)]
    part = across(terms.reshape(8, 4 * ROWS, width), blocks)
    joined = pl.pallas_call(
        join_kernel,
        name="join",
        compiler_params=params(6),
        out_shape=shape((4, ROWS, width), bf16),
        in_specs=[VM],
        out_specs=VM,
    )(part.reshape(8, 4, ROWS, width))
    arrived = across(joined, strides)
    h, squares = pl.pallas_call(
        hidden_kernel,
        name="hidden",
        compiler_params=params(6),
        out_shape=(shape((ROWS, width), f32), shape((count, STAT, HD), bf16)),
        in_specs=[VM, VM],
        out_specs=(VM, VM),
    )(arrived, residual)
    totals = to_all(squares)
    draft, layer_out = pl.pallas_call(
        draft_kernel,
        name="draft",
        compiler_params=params(4),
        out_shape=(shape((REQ * MAXACC, width), bf16), shape((ROWS, width), bf16)),
        in_specs=[VM, VM, VM, VM],
        out_specs=(VM, VM),
    )(totals, h, gains, sel)
    return (layer_out, draft.reshape(REQ, MAXACC, width))


def solution(mesh):
    return jax.shard_map(
        on_device,
        mesh=mesh,
        in_specs=(
            P("dp", "tensor"),
            P("dp", "tensor", None),
            P("dp", "tensor", None),
            P("dp", None, None),
            P("dp", None, None),
            P("dp", "tensor"),
            P("tensor", None),
            P("tensor"),
            P("dp", None),
            P("dp"),
            P("dp"),
        ),
        out_specs=(P("dp", "tensor"), P("dp", None, "tensor")),
        check_vma=False,
    )
```

```python
import jax
import jax.numpy as jnp
from jax import lax
from jax.experimental import pallas as pl
from jax.experimental.pallas import tpu as pltpu
from jax.sharding import PartitionSpec as P

D = 8192
HD = 128
KVH = 4
TREE = 16
REQ = 4
ROWS = REQ * TREE
MAXACC = 8
HEADS = 32
GROUP = HEADS // KVH
STAT = 8
MSG = ROWS + STAT

floor_score = -1e30
epsilon = 1e-05
score_scale = HD ** (-0.5)
f32 = jnp.float32
bf16 = jnp.bfloat16
VM = pl.BlockSpec(memory_space=pltpu.VMEM)
SM = pl.BlockSpec(memory_space=pltpu.SMEM)
STAGGER = 9600


def iota(shape, dim):
    return lax.broadcasted_iota(jnp.int32, shape, dim)


def three_parts(x):
    hi = x.astype(bf16).astype(f32)
    mid = (x - hi).astype(bf16).astype(f32)
    return hi, mid, x - hi - mid


def to_all(x):
    return lax.all_to_all(x, "tensor", split_axis=0, concat_axis=0, tiled=True)


def spread_kernel(late, q, out):
    @pl.when(late[0] > 0)
    def _():
        pl.delay(STAGGER)

    for d in range(out.shape[0]):
        out[d] = q[...]


def across(x, groups):
    return lax.all_to_all(
        x, "tensor", split_axis=0, concat_axis=0, axis_index_groups=groups, tiled=True
    )


def tree_kernel(
    rank, parents, acc_node, cache_len, q, kt, vt, k, v, gain,
    o_ref, lse_ref, sel_ref, left_ref, gain_ref,
):
    gain_ref[...] = jnp.broadcast_to(gain[...].astype(f32), gain_ref.shape)
    for r in range(REQ):
        left_ref[r] = jnp.full((8, HD), cache_len[r] - rank[0] * k.shape[1], jnp.int32)
    row = iota((ROWS, ROWS), 0)
    col = iota((ROWS, ROWS), 1)
    same = (row // TREE) == (col // TREE)
    up = jnp.zeros((ROWS, ROWS), jnp.int32)
    for r in range(REQ):
        for i in range(1, TREE):
            up = jnp.where(row == r * TREE + i, parents[r, i] + r * TREE, up)
    link = jnp.where((up == col) & (row % TREE > 0), 1.0, 0.0)
    reach = jnp.where(row == col, 1.0, link)
    for sweep in range((TREE - 1).bit_length()):
        half = reach.astype(bf16)
        reach = jnp.minimum(jnp.dot(half, half, preferred_element_type=f32), 1.0)
    lane = pl.ds(pl.multiple_of((rank[0] // GROUP) * HD, HD), HD)
    keys = jnp.concatenate([kt[r, :, lane] for r in range(REQ)], axis=0)
    values = jnp.concatenate([vt[r, :, lane] for r in range(REQ)], axis=0)
    nt = (((1,), (1,)), ((), ()))
    scores = lax.dot_general(q[...], keys, nt, preferred_element_type=f32) * score_scale
    valid = (reach > 0.5) & same
    scores = jnp.where(valid, scores, floor_score)
    top = jnp.max(scores, axis=1, keepdims=True)
    e = jnp.where(valid, jnp.exp(scores - top), 0.0)
    total = jnp.sum(e, axis=1, keepdims=True)
    o_ref[...] = jnp.dot(e.astype(bf16), values, preferred_element_type=f32) / total
    lse = jnp.broadcast_to(top + jnp.log(total), (ROWS, HD))
    lse_ref[...] = lse.T[:8, :]
    depth = lax.dot_general(
        jnp.ones((8, ROWS), bf16), reach.astype(bf16), nt, preferred_element_type=f32
    )[:1, :] - 1.0
    out = iota((REQ * MAXACC, ROWS), 0)
    lanes = iota((REQ * MAXACC, ROWS), 1)
    chosen = jnp.zeros((REQ * MAXACC, ROWS), jnp.int32)
    for r in range(REQ):
        chosen = jnp.where(out // MAXACC == r, acc_node[r] + r * TREE, chosen)
    onehot = jnp.where(lanes == chosen, 1.0, 0.0).astype(bf16)
    onpath = jnp.dot(onehot, reach.astype(bf16), preferred_element_type=f32)
    level = (out % MAXACC).astype(f32)
    sel_ref[...] = jnp.where(depth == level, onpath, 0.0).astype(bf16)


def attend_kernel(left, q, k, v, out):
    span = k.shape[1]
    nt = (((1,), (1,)), ((), ()))
    tn = (((0,), (0,)), ((), ()))
    pos = iota((span, HD), 0)
    sub = iota((GROUP, HD), 0)
    lane = iota((GROUP, HD), 1)
    packed = [jnp.zeros((GROUP, HD), f32)] * KVH
    for g in range(KVH):
        for r in range(REQ):
            rows = slice(r * TREE, (r + 1) * TREE)
            valid = pos < left[r, 0:1, :]
            cols = slice(g * HD, (g + 1) * HD)
            heads = slice(g * GROUP, (g + 1) * GROUP)
            qh = q[heads, rows, :].reshape(GROUP * TREE, HD)
            s = lax.dot_general(k[r, :, cols], qh, nt, preferred_element_type=f32) * score_scale
            s = jnp.where(valid, s, floor_score)
            top = jnp.max(s, axis=0, keepdims=True)
            e = jnp.exp(s - top)
            total = jnp.sum(e, axis=0, keepdims=True)
            some = left[r, 0:1, :] > 0
            inv = jnp.where(some, 1.0 / total, 0.0)
            lse = jnp.where(some, top + jnp.log(total), floor_score)
            p = (e * inv).astype(bf16)
            o = lax.dot_general(p, v[r, :, cols], tn, preferred_element_type=f32)
            out[heads, rows, :] = o.astype(bf16).reshape(GROUP, TREE, HD)
            turned = pltpu.roll(
                jnp.broadcast_to(pltpu.roll(lse, (r + 1) * TREE, 1), (GROUP, HD)),
                0,
                1,
                stride=TREE,
                stride_axis=0,
            )
            packed[g] = jnp.where(lane // TREE == r, turned, packed[g])
    for g in range(KVH):
        hi, mid, lo = three_parts(packed[g])
        first = jnp.where(lane < ROWS, hi, pltpu.roll(mid, ROWS, 1))
        for j in range(GROUP):
            i = GROUP - 1 - j
            stat = jnp.where(sub == 0, first[i : i + 1, :], jnp.where(sub == 1, lo[i : i + 1, :], 0.0))
            out[g * GROUP + j, ROWS:MSG, :] = stat.astype(bf16)


def project_kernel(got, o_tree, lse_tree, wo, out):
    srcs = got.shape[0]
    stats = got[:, ROWS:MSG, :].astype(f32)
    first = stats[:, 0, :]
    lse = first + pltpu.roll(first, ROWS, 1) + stats[:, 1, :]
    tree = lse_tree[0:1, :]
    tree = jnp.concatenate([tree, jnp.zeros((1, HD - ROWS), f32)], axis=1)
    top = jnp.maximum(jnp.max(lse, axis=0, keepdims=True), tree)
    w = jnp.exp(lse - top)
    wt = jnp.exp(tree - top)
    inv = 1.0 / (jnp.sum(w, axis=0, keepdims=True) + wt)
    every = jnp.concatenate(
        [w * inv, jnp.broadcast_to(wt * inv, (8, HD)), jnp.zeros((HD - srcs - 8, HD), f32)], axis=0
    ).T[:ROWS, :]
    att = o_tree[...] * every[:, srcs : srcs + 1]
    for c in range(srcs):
        att = att + got[c, :ROWS, :].astype(f32) * every[:, c : c + 1]
    att = att.astype(bf16)
    width = out.shape[2]
    for d in range(out.shape[0]):
        part = jnp.dot(att, wo[:, d * width : (d + 1) * width], preferred_element_type=f32)
        x, y = d // 8, d % 8
        out[x * 8 + (y % 2) * 4 + y // 2] = part.astype(bf16)


def join_kernel(got, out):
    for d in range(out.shape[0]):
        total = got[0, d].astype(f32)
        for c in range(1, got.shape[0]):
            total = total + got[c, d].astype(f32)
        out[d] = total.astype(bf16)


def hidden_kernel(got, residual, h_ref, sq_ref):
    h = residual[...].astype(f32)
    for c in range(got.shape[0]):
        h = h + got[c].astype(f32)
    h_ref[...] = h
    sq = h * h
    part = sq[:, :HD]
    for c in range(HD, sq.shape[1], HD):
        part = part + sq[:, c : c + HD]
    row = jnp.sum(part.T, axis=0, keepdims=True)
    row = jnp.concatenate([row, jnp.zeros((1, HD - ROWS), f32)], axis=1)
    hi, mid, lo = three_parts(row)
    sub = iota((STAT, HD), 0)
    tile = jnp.where(sub == 0, hi, jnp.where(sub == 1, mid, jnp.where(sub == 2, lo, 0.0))).astype(bf16)
    for c in range(sq_ref.shape[0]):
        sq_ref[c] = tile


def draft_kernel(got, h, gain, sel, out, layer_ref):
    layer_ref[...] = h[...].astype(bf16)
    tile = got[0].astype(f32)
    for c in range(1, got.shape[0]):
        tile = tile + got[c].astype(f32)
    total = jnp.sum(tile, axis=0, keepdims=True)
    scale = lax.rsqrt(jnp.broadcast_to(total / D, (HD, HD)).T[:ROWS, :] + epsilon)
    for c in range(0, h.shape[1], HD):
        cols = slice(c, c + HD)
        feat = (h[:, cols] * scale * gain[0:1, cols]).astype(bf16)
        out[:, cols] = jnp.dot(sel[...], feat, preferred_element_type=f32).astype(bf16)


def params(mib):
    return pltpu.CompilerParams(vmem_limit_bytes=mib * 2**20)


def shape(dims, kind):
    return jax.ShapeDtypeStruct(dims, kind)


def on_device(
    q_rows,
    k_cache,
    v_cache,
    k_tree,
    v_tree,
    residual,
    wo_rows,
    gain,
    parents,
    cache_len,
    accepted_node,
):
    count = lax.axis_size("tensor")
    rank = lax.axis_index("tensor").astype(jnp.int32).reshape(1)
    width = residual.shape[1]
    q_each = pl.pallas_call(
        spread_kernel,
        name="spread",
        compiler_params=params(2),
        out_shape=shape((count, ROWS, HD), bf16),
        in_specs=[SM, VM],
        out_specs=VM,
    )(lax.axis_index("dp").astype(jnp.int32).reshape(1) % 2, q_rows)
    q_all = to_all(q_each)
    o_tree, lse_tree, sel, left, gains = pl.pallas_call(
        tree_kernel,
        name="tree",
        compiler_params=params(6),
        out_shape=(
            shape((ROWS, HD), f32),
            shape((8, ROWS), f32),
            shape((REQ * MAXACC, ROWS), bf16),
            shape((REQ, 8, HD), jnp.int32),
            shape((8, width), f32),
        ),
        in_specs=[SM, SM, SM, SM, VM, VM, VM, VM, VM, VM],
        out_specs=(VM, VM, VM, VM, VM),
        cost_estimate=pl.CostEstimate(flops=10**8, bytes_accessed=4 * 10**6, transcendentals=10000),
    )(
        rank, parents, accepted_node, cache_len, q_rows, k_tree, v_tree, k_cache, v_cache,
        gain.reshape(1, width),
    )
    sent = pl.pallas_call(
        attend_kernel,
        name="attend",
        compiler_params=params(10),
        out_shape=shape((HEADS, MSG, HD), bf16),
        in_specs=[VM, VM, VM, VM],
        out_specs=VM,
    )(left, q_all, k_cache, v_cache)
    got = to_all(sent)
    terms = pl.pallas_call(
        project_kernel,
        name="project",
        compiler_params=params(10),
        out_shape=shape((count, ROWS, width), bf16),
        in_specs=[VM, VM, VM, VM],
        out_specs=VM,
    )(got, o_tree, lse_tree, wo_rows)
    blocks = [[x * 8 + 2 * b + a for x in range(4) for a in range(2)] for b in range(4)]
    strides = [[x * 8 + 2 * b + a for b in range(4)] for x in range(4) for a in range(2)]
    part = across(terms.reshape(8, 4 * ROWS, width), blocks)
    joined = pl.pallas_call(
        join_kernel,
        name="join",
        compiler_params=params(6),
        out_shape=shape((4, ROWS, width), bf16),
        in_specs=[VM],
        out_specs=VM,
    )(part.reshape(8, 4, ROWS, width))
    arrived = across(joined, strides)
    h, squares = pl.pallas_call(
        hidden_kernel,
        name="hidden",
        compiler_params=params(6),
        out_shape=(shape((ROWS, width), f32), shape((count, STAT, HD), bf16)),
        in_specs=[VM, VM],
        out_specs=(VM, VM),
    )(arrived, residual)
    totals = to_all(squares)
    draft, layer_out = pl.pallas_call(
        draft_kernel,
        name="draft",
        compiler_params=params(4),
        out_shape=(shape((REQ * MAXACC, width), bf16), shape((ROWS, width), bf16)),
        in_specs=[VM, VM, VM, VM],
        out_specs=(VM, VM),
    )(totals, h, gains, sel)
    return (layer_out, draft.reshape(REQ, MAXACC, width))


def solution(mesh):
    return jax.shard_map(
        on_device,
        mesh=mesh,
        in_specs=(
            P("dp", "tensor"),
            P("dp", "tensor", None),
            P("dp", "tensor", None),
            P("dp", None, None),
            P("dp", None, None),
            P("dp", "tensor"),
            P("tensor", None),
            P("tensor"),
            P("dp", None),
            P("dp"),
            P("dp"),
        ),
        out_specs=(P("dp", "tensor"), P("dp", None, "tensor")),
        check_vma=False,
    )
```
